32 devices in a mesh: tm: 32 (over z, y, x, core).
Axes of the slice: x: 2, y: 2, z: 4, core: 2. Of those that a mesh axis runs over, the one named last changes fastest.
Arguments:
- signal: bfloat16 [8192, 512], P('tm'), may hold values from -18 to 18
- conv_weight: bfloat16 [1024, 2048], replicated
- attn_gain: float32 [2048], replicated, may hold values from 0.1 to 1.9
- w_query: bfloat16 [2048, 1024], replicated, may hold values from -0.125 to 0.125
- w_keyval: bfloat16 [2048, 512], replicated, may hold values from -0.125 to 0.125
- w_out: bfloat16 [1024, 2048], replicated, may hold values from -0.1875 to 0.1875
- head_scale: float32 [8], replicated, as said below
- ffn_gain: float32 [2048], replicated, may hold values from 0.1 to 1.9
- router_w: bfloat16 [2048, 64], replicated, may hold values from -0.125 to 0.125
- expert_in: bfloat16 [2, 90112, 2048], P(None, 'tm'), may hold values from -0.125 to 0.125
- expert_out: bfloat16 [90112, 2048], P('tm'), may hold values from -0.15625 to 0.15625
- expert_ids: int32 [8192, 2], P('tm'), may hold values from 0 to 63, as said below
- slot_ids: int32 [8192, 2], P('tm'), may hold values from 0 to 15, as said below
Outputs:
- layer_output: bfloat16 [8192, 2048], P('tm')
The draws below stay inside these ranges and needn't reach their ends.
Inputs may be any that keep to these rules, and one draw needn't show every extreme that they name: `head_scale`: each head's scale lies between 0.5 and 64. `expert_ids`: the two experts of a token differ. Among the 256 tokens of one device no expert is named more than 16 times, and some expert is named exactly 16 times by the tokens of every device. `slot_ids`: routes of one device's tokens that name the same expert have different slots.
All inputs are finite; a program needn't handle non-finite values.
Results may differ from the reference program's by a relative error of at most 0.019.
Values may be sent and summed in bfloat16 or wider, within the bound.
No kernel may reach another device: no remote copies, remote signals or barrier semaphores. Data moves between devices by JAX's collectives and lax.ppermute only.
A program may use at most 192 MiB of HBM per device.

```python
import math
import jax
import jax.numpy as jnp
from jax import lax

D = 2048
FF = 1408
EXPERTS = 64
HEADS = 8
KV_HEADS = 2
HEAD_DIM = 128
WINDOW = 2048
TOK_DEV = 256
PATCH_DIM = 512
TOKENS = 8192
CAP = 16
COPIES = 1
N_TM = 32


def draw_signal(key, part):
    key_noise, key_rows = jax.random.split(key, 2)
    row_scale = jnp.exp(jax.random.uniform(key_rows, (TOKENS, 1), jnp.float32, math.log(0.3), math.log(3.0)))
    noise_vals = jnp.clip(jax.random.normal(key_noise, (TOKENS, PATCH_DIM), jnp.float32), -6.0, 6.0)
    values = noise_vals * row_scale
    return values.astype(jnp.bfloat16)


def draw_conv_weight(key, part):
    key_vals, key_cols = jax.random.split(key, 2)
    col_scale = jnp.exp(jax.random.uniform(key_cols, (1, D), jnp.float32, math.log(0.3), math.log(3.0)))
    noise_vals = jnp.clip(jax.random.normal(key_vals, (2 * PATCH_DIM, D), jnp.float32), -4.0, 4.0)
    return (noise_vals * col_scale * (2.0 * PATCH_DIM) ** (-0.5)).astype(jnp.bfloat16)


def draw_head_scale(key, part):
    low_end, high_end = (0.5, 4.0)
    return jnp.exp(jax.random.uniform(key, (HEADS,), jnp.float32, math.log(low_end), math.log(high_end)))


def route_tables(key):
    blocks = TOKENS // TOK_DEV
    subkeys = jax.random.split(key, 6)
    favored = jax.random.randint(subkeys[0], (), 0, EXPERTS)
    expert_row = jnp.arange(EXPERTS, dtype=jnp.int32)
    ranking = jax.random.randint(subkeys[1], (blocks, EXPERTS), 0, 1 << 16) * EXPERTS + expert_row[None, :]
    ranking = jnp.where(expert_row[None, :] == favored, -1, ranking)
    expert_order = jnp.argsort(ranking, axis=1)
    hot_count = EXPERTS // 8 + jax.random.randint(subkeys[2], (blocks, 1), 0, EXPERTS // 16 + 1)
    is_cold = expert_row[None, :] >= hot_count
    share_weight = jnp.where(is_cold, jax.random.randint(subkeys[3], (blocks, EXPERTS), 1, 3), 0)
    remain = 2 * TOK_DEV - CAP * hot_count
    share_total = jnp.sum(share_weight, axis=1, keepdims=True)
    share_cum = jnp.cumsum(share_weight, axis=1)
    upper_cut = remain * share_cum // share_total
    lower_cut = remain * (share_cum - share_weight) // share_total
    quota_rank = jnp.where(is_cold, upper_cut - lower_cut, CAP)
    rank_match = expert_order[:, :, None] == expert_row[None, None, :]
    quota_exp = jnp.sum(jnp.where(rank_match, quota_rank[:, :, None], 0), axis=1)
    run_ends = jnp.cumsum(quota_exp, axis=1)
    run_starts = run_ends - quota_exp
    tickets = jnp.arange(2 * TOK_DEV, dtype=jnp.int32)
    ticket_expert = jnp.sum((run_ends[:, None, :] <= tickets[None, :, None]).astype(jnp.int32), axis=2)
    rank_in = tickets[None, :] - jnp.take_along_axis(run_starts, ticket_expert, axis=1)
    slot_keys = jax.random.randint(subkeys[4], (blocks, EXPERTS, CAP), 0, 1 << 16) * CAP + jnp.arange(CAP, dtype=jnp.int32)
    slot_perm = jnp.argsort(slot_keys, axis=2).reshape(blocks, EXPERTS * CAP)
    ticket_slot = jnp.take_along_axis(slot_perm, ticket_expert * CAP + rank_in, axis=1)
    token_keys = jax.random.randint(subkeys[5], (blocks, TOK_DEV), 0, 1 << 16) * TOK_DEV + jnp.arange(TOK_DEV, dtype=jnp.int32)
    token_perm = jnp.argsort(token_keys, axis=1)
    ids_first = jnp.take_along_axis(ticket_expert, token_perm, axis=1)
    ids_second = jnp.take_along_axis(ticket_expert, token_perm + TOK_DEV, axis=1)
    slot_first = jnp.take_along_axis(ticket_slot, token_perm, axis=1)
    slot_second = jnp.take_along_axis(ticket_slot, token_perm + TOK_DEV, axis=1)
    expert_table = jnp.stack([ids_first, ids_second], axis=-1).reshape(TOKENS, 2).astype(jnp.int32)
    slot_table = jnp.stack([slot_first, slot_second], axis=-1).reshape(TOKENS, 2).astype(jnp.int32)
    return (expert_table, slot_table)


def draw_expert_ids(key, part):
    return route_tables(jax.random.fold_in(key, 11))[0]


def draw_slot_ids(key, part):
    return route_tables(jax.random.fold_in(key, 11))[1]


def level_of(key, extent, shards, least, high):
    def one(dim, shards_of):
        steps = jax.random.uniform(jax.random.fold_in(jax.random.fold_in(key, 6), dim), (shards_of,), jnp.float32, least / len(shards), high / len(shards))
        return jnp.repeat(jnp.exp(steps), extent[dim] // shards_of).reshape((-1,) + (1,) * (len(extent) - dim - 1))

    level = one(*shards[0])
    for cut in shards[1:]:
        level = level * one(*cut)
    return level


def noise(key, extent, width, limit, cuts=(), kind=jnp.bfloat16):
    result = width * jax.random.normal(key, extent, jnp.float32)
    if cuts:
        result = result * level_of(key, extent, cuts, -0.22, 0.18)
    return jnp.clip(result, -limit, limit).astype(kind)


def setup_inputs(seed: int = 0) -> dict:
    splits = jax.random.split(jax.random.key(seed), 14)
    return {
        "signal": draw_signal(jax.random.fold_in(splits[13], 71), 0),
        "conv_weight": draw_conv_weight(jax.random.fold_in(splits[13], 71), 0),
        "attn_gain": jnp.clip(1.0 + 0.18 * jax.random.normal(splits[2], (D,), jnp.float32), 0.1, 1.9),
        "w_query": noise(splits[3], (D, HEADS * HEAD_DIM), D ** -0.5, 0.125),
        "w_keyval": noise(splits[4], (D, 2 * KV_HEADS * HEAD_DIM), D ** -0.5, 0.125),
        "w_out": noise(splits[5], (HEADS * HEAD_DIM, D), (HEADS * HEAD_DIM) ** -0.5, 0.1875),
        "head_scale": draw_head_scale(jax.random.fold_in(splits[13], 71), 0),
        "ffn_gain": jnp.clip(1.0 + 0.18 * jax.random.normal(splits[7], (D,), jnp.float32), 0.1, 1.9),
        "router_w": noise(splits[8], (D, EXPERTS), D ** -0.5, 0.125),
        "expert_in": noise(splits[9], (2, EXPERTS * FF, D), D ** -0.5, 0.125, ((1, 32),)),
        "expert_out": noise(splits[10], (EXPERTS * FF, D), FF ** -0.5, 0.15625, ((0, 32),)),
        "expert_ids": draw_expert_ids(jax.random.fold_in(splits[13], 71), 0),
        "slot_ids": draw_slot_ids(jax.random.fold_in(splits[13], 71), 0),
    }


NORM_EPS = 1e-06
MASKED = -1e+30

def rms_scale(values, gain_vec):
    mean_sq = lax.optimization_barrier(jnp.mean(values * values, axis=-1, keepdims=True))
    return values * lax.rsqrt(mean_sq + NORM_EPS) * gain_vec

def head_norm(values):
    mean_sq = lax.optimization_barrier(jnp.mean(values * values, axis=-1, keepdims=True))
    return values * lax.rsqrt(mean_sq + NORM_EPS)

def reference(signal, conv_weight, attn_gain, w_query, w_keyval, w_out, head_scale, ffn_gain, router_w, expert_in, expert_out, expert_ids, slot_ids):
    previous = jnp.concatenate([jnp.zeros((1, signal.shape[1]), signal.dtype), signal[:-1]], axis=0)
    patch_pairs = jnp.concatenate([previous, signal], axis=1)
    embedded = jnp.dot(patch_pairs, conv_weight, preferred_element_type=jnp.float32).astype(jnp.bfloat16)
    normed = rms_scale(embedded.astype(jnp.float32), attn_gain).astype(jnp.bfloat16)
    group_size = HEADS // KV_HEADS
    queries = jnp.dot(normed, w_query, preferred_element_type=jnp.float32).reshape(TOKENS, KV_HEADS, group_size, HEAD_DIM)
    keyval = jnp.dot(normed, w_keyval, preferred_element_type=jnp.float32).reshape(TOKENS, 2, KV_HEADS, HEAD_DIM)
    query_unit = head_norm(queries).astype(jnp.bfloat16)
    key_unit = head_norm(keyval[:, 0]).astype(jnp.bfloat16)
    value_bf = keyval[:, 1].astype(jnp.bfloat16)
    block_rows = math.gcd(TOKENS, 512)
    key_pad = jnp.concatenate([jnp.zeros((WINDOW, KV_HEADS, HEAD_DIM), key_unit.dtype), key_unit], axis=0)
    value_pad = jnp.concatenate([jnp.zeros((WINDOW, KV_HEADS, HEAD_DIM), value_bf.dtype), value_bf], axis=0)
    score_scale = head_scale.reshape(KV_HEADS, group_size, 1, 1) / math.sqrt(HEAD_DIM)

    def attend(block_start):
        query_blk = lax.dynamic_slice_in_dim(query_unit, block_start, block_rows, 0)
        key_blk = lax.dynamic_slice_in_dim(key_pad, block_start, WINDOW + block_rows, 0)
        value_blk = lax.dynamic_slice_in_dim(value_pad, block_start, WINDOW + block_rows, 0)
        scores = jnp.einsum('qkgd,lkd->kgql', query_blk.astype(jnp.float32), key_blk.astype(jnp.float32))
        scores = scores * score_scale
        query_pos = block_start + jnp.arange(block_rows, dtype=jnp.int32)
        key_pos = block_start - WINDOW + jnp.arange(WINDOW + block_rows, dtype=jnp.int32)
        visible = (key_pos[None, :] <= query_pos[:, None]) & (key_pos[None, :] > query_pos[:, None] - WINDOW) & (key_pos[None, :] >= 0)
        scores = jnp.where(visible, scores, MASKED)
        row_max = lax.optimization_barrier(jnp.max(scores, axis=-1, keepdims=True))
        exp_scores = jnp.exp(scores - row_max)
        probs = (exp_scores / lax.optimization_barrier(jnp.sum(exp_scores, axis=-1, keepdims=True))).astype(jnp.bfloat16)
        context = jnp.einsum('kgql,lkd->qkgd', probs.astype(jnp.float32), value_blk.astype(jnp.float32))
        return context.astype(jnp.bfloat16).reshape(block_rows, HEADS * HEAD_DIM)
    starts = jnp.arange(TOKENS // block_rows, dtype=jnp.int32) * block_rows
    context = lax.map(attend, starts).reshape(TOKENS, HEADS * HEAD_DIM)
    stream_mid = (embedded.astype(jnp.float32) + jnp.dot(context, w_out, preferred_element_type=jnp.float32)).astype(jnp.bfloat16)
    ffn_input = rms_scale(stream_mid.astype(jnp.float32), ffn_gain).astype(jnp.bfloat16)
    affinity = jax.nn.sigmoid(jnp.dot(ffn_input, router_w, preferred_element_type=jnp.float32))
    picked = jnp.take_along_axis(affinity, expert_ids, axis=1)
    route_weight = picked / lax.optimization_barrier(jnp.sum(picked, axis=1, keepdims=True))
    source_dev = jnp.arange(TOKENS, dtype=jnp.int32) // TOK_DEV
    flat_index = (expert_ids * N_TM + source_dev[:, None]) * CAP + slot_ids
    dispatched = jnp.zeros((EXPERTS * N_TM * CAP, D), jnp.bfloat16)
    dispatched = dispatched.at[flat_index[:, 0]].set(ffn_input).at[flat_index[:, 1]].set(ffn_input)
    dispatched = dispatched.reshape(EXPERTS, N_TM * CAP, D)
    w_in_all = expert_in.reshape(2, EXPERTS, FF, D)
    w_out_all = expert_out.reshape(EXPERTS, FF, D)
    part_units = FF // COPIES

    def run_expert(expert):
        rows_in = lax.dynamic_index_in_dim(dispatched, expert, 0, keepdims=False)
        w_in_one = lax.dynamic_index_in_dim(w_in_all, expert, 1, keepdims=False)
        w_out_one = lax.dynamic_index_in_dim(w_out_all, expert, 0, keepdims=False)
        partial_sum = jnp.zeros((N_TM * CAP, D), jnp.float32)
        for part_idx in range(COPIES):
            low_unit = part_idx * part_units
            gate_act = jnp.dot(rows_in, w_in_one[0, low_unit:low_unit + part_units].T, preferred_element_type=jnp.float32)
            up_act = jnp.dot(rows_in, w_in_one[1, low_unit:low_unit + part_units].T, preferred_element_type=jnp.float32)
            hidden = (jax.nn.silu(gate_act) * up_act).astype(jnp.bfloat16)
            piece = jnp.dot(hidden, w_out_one[low_unit:low_unit + part_units], preferred_element_type=jnp.float32).astype(jnp.bfloat16)
            partial_sum = partial_sum + lax.optimization_barrier(piece).astype(jnp.float32)
        return partial_sum.astype(jnp.bfloat16)
    outputs = lax.map(run_expert, jnp.arange(EXPERTS, dtype=jnp.int32))
    flat_out = outputs.reshape(EXPERTS * N_TM * CAP, D)
    route_first = flat_out[flat_index[:, 0]].astype(jnp.float32)
    route_second = flat_out[flat_index[:, 1]].astype(jnp.float32)
    mixed_rows = stream_mid.astype(jnp.float32) + route_weight[:, 0:1] * route_first + route_weight[:, 1:2] * route_second
    return mixed_rows.astype(jnp.bfloat16)
```

```python
import functools
import math

import jax
import jax.numpy as jnp
from jax import lax
from jax.experimental import pallas as pl
from jax.experimental.pallas import tpu as pltpu
from jax.sharding import PartitionSpec as P

HEAD_DIM = 128
WINDOW = 2048
CAP = 16

NORM_EPS = 1e-06
MASKED = -1e30


def from_behind(block, axis, distance):
    devices = range(lax.axis_size(axis))
    route = [(i - distance, i) for i in devices if i - distance in devices]
    return lax.ppermute(block, axis, route)


def rms_scale(values, gain_vec):
    mean_sq = jnp.mean(values * values, axis=-1, keepdims=True)
    return values * lax.rsqrt(mean_sq + NORM_EPS) * gain_vec


def head_norm(values):
    mean_sq = jnp.mean(values * values, axis=-1, keepdims=True)
    return values * lax.rsqrt(mean_sq + NORM_EPS)


def expert_body(steps, rows_ref, w_in_ref, w_out_ref, out_ref, total_ref):
    step = pl.program_id(1)
    width = w_in_ref.shape[1]
    rows = rows_ref[...]
    nt = (((1,), (1,)), ((), ()))
    gate = lax.dot_general(rows, w_in_ref[0], nt, preferred_element_type=jnp.float32)
    up = lax.dot_general(rows, w_in_ref[1], nt, preferred_element_type=jnp.float32)
    hidden = (gate / (1.0 + jnp.exp(-gate)) * up).astype(jnp.bfloat16)
    part = jnp.dot(hidden, w_out_ref[...], preferred_element_type=jnp.float32)

    @pl.when(step == 0)
    def _():
        total_ref[...] = part

    @pl.when(step > 0)
    def _():
        total_ref[...] += part

    @pl.when(step == steps - 1)
    def _():
        out_ref[...] = total_ref[...].astype(out_ref.dtype)


def run_expert(rows, expert_in, expert_out, local, local_count):
    row_total, feat_dim = rows.shape
    units = expert_out.shape[0] // local_count
    width = 352
    steps = units // width
    first = local * steps
    tile = math.gcd(row_total, 512)
    flops = 6 * row_total * units * feat_dim
    return pl.pallas_call(
        functools.partial(expert_body, steps),
        grid=(row_total // tile, steps),
        in_specs=[
            pl.BlockSpec((tile, feat_dim), lambda r, i: (r, 0)),
            pl.BlockSpec((2, width, feat_dim), lambda r, i: (0, first + i, 0)),
            pl.BlockSpec((width, feat_dim), lambda r, i: (first + i, 0)),
        ],
        out_specs=pl.BlockSpec((tile, feat_dim), lambda r, i: (r, 0)),
        out_shape=jax.ShapeDtypeStruct((row_total, feat_dim), jnp.bfloat16),
        scratch_shapes=[pltpu.VMEM((tile, feat_dim), jnp.float32)],
        compiler_params=pltpu.CompilerParams(vmem_limit_bytes=40 << 20),
        cost_estimate=pl.CostEstimate(
            flops=flops,
            bytes_accessed=6 * units * feat_dim + 4 * row_total * feat_dim,
            transcendentals=row_total * units,
        ),
    )(rows, expert_in, expert_out)


def shards(
    signal,
    conv_weight,
    attn_gain,
    w_query,
    w_keyval,
    w_out,
    head_scale,
    ffn_gain,
    router_w,
    expert_in,
    expert_out,
    expert_ids,
    slot_ids,
):
    row_count = signal.shape[0]
    feat_dim = conv_weight.shape[1]
    devices = lax.axis_size("tm")
    dev_index = lax.axis_index("tm")
    experts = router_w.shape[1]
    copies = max(devices // experts, 1)
    local_count = max(experts // devices, 1)
    slots = devices * CAP

    route_key = expert_ids * CAP + slot_ids
    row_id = jnp.arange(slots, dtype=jnp.int32)
    row_dev, row_slot = row_id // CAP, row_id % CAP
    row_keys = [
        (row_dev // copies * local_count + local) * CAP + row_slot for local in range(local_count)
    ]

    def spread(values, local):
        hot = (row_keys[local][:, None] == route_key[None, :, 0]) | (
            row_keys[local][:, None] == route_key[None, :, 1]
        )
        return jnp.dot(
            hot.astype(jnp.bfloat16), values, preferred_element_type=jnp.float32
        ).astype(jnp.bfloat16)

    def exchange(rows):
        return lax.all_to_all(rows, "tm", split_axis=0, concat_axis=0, tiled=True)

    before = from_behind(signal[row_count - 1 :], "tm", 1)
    previous = jnp.concatenate([before, signal[:-1]], axis=0)
    patch_pairs = jnp.concatenate([previous, signal], axis=1)
    pairs_out = jnp.concatenate(
        [spread(patch_pairs, local).reshape(devices, CAP, -1) for local in range(local_count)],
        axis=1,
    )
    pairs_in = exchange(pairs_out)

    embedded = jnp.dot(patch_pairs, conv_weight, preferred_element_type=jnp.float32).astype(
        jnp.bfloat16
    )
    normed = rms_scale(embedded.astype(jnp.float32), attn_gain).astype(jnp.bfloat16)
    head_count = head_scale.shape[0]
    kv_dim = w_keyval.shape[1] // 2
    kv_heads = kv_dim // HEAD_DIM
    group_size = head_count // kv_heads
    keyval = jnp.dot(normed, w_keyval, preferred_element_type=jnp.float32).reshape(
        row_count, 2, kv_heads, HEAD_DIM
    )
    key_unit = head_norm(keyval[:, 0]).astype(jnp.bfloat16)
    value_bf = keyval[:, 1].astype(jnp.bfloat16)
    own_kv = jnp.concatenate(
        [key_unit.reshape(row_count, kv_dim), value_bf.reshape(row_count, kv_dim)], axis=1
    )
    reach_blocks = WINDOW // row_count
    earlier = [from_behind(own_kv, "tm", distance) for distance in range(reach_blocks, 0, -1)]
    queries = jnp.dot(normed, w_query, preferred_element_type=jnp.float32).reshape(
        row_count, kv_heads, group_size, HEAD_DIM
    )
    query_unit = head_norm(queries).astype(jnp.bfloat16)
    window_kv = jnp.concatenate(earlier + [own_kv], axis=0)
    key_len = window_kv.shape[0]
    win_keys = window_kv[:, :kv_dim].reshape(key_len, kv_heads, HEAD_DIM)
    win_values = window_kv[:, kv_dim:].reshape(key_len, kv_heads, HEAD_DIM)
    scores = jnp.einsum("qkgd,lkd->kgql", query_unit, win_keys, preferred_element_type=jnp.float32)
    scores = scores * (head_scale.reshape(kv_heads, group_size, 1, 1) / math.sqrt(HEAD_DIM))
    query_pos = dev_index * row_count + jnp.arange(row_count, dtype=jnp.int32)
    key_pos = (dev_index - reach_blocks) * row_count + jnp.arange(key_len, dtype=jnp.int32)
    visible = (
        (key_pos[None, :] <= query_pos[:, None])
        & (key_pos[None, :] > query_pos[:, None] - WINDOW)
        & (key_pos[None, :] >= 0)
    )
    scores = jnp.where(visible, scores, MASKED)
    row_max = jnp.max(scores, axis=-1, keepdims=True)
    exp_scores = jnp.exp(scores - row_max)
    probs = (exp_scores / jnp.sum(exp_scores, axis=-1, keepdims=True)).astype(jnp.bfloat16)
    context = jnp.einsum("kgql,lkd->qkgd", probs, win_values, preferred_element_type=jnp.float32)
    context = context.astype(jnp.bfloat16).reshape(row_count, head_count * HEAD_DIM)

    context_in = [
        exchange(spread(context, local).reshape(devices, CAP, -1)) for local in range(local_count)
    ]

    def rows_of(pairs, contexts):
        placed = jnp.dot(pairs, conv_weight, preferred_element_type=jnp.float32).astype(
            jnp.bfloat16
        )
        mid = (
            placed.astype(jnp.float32)
            + jnp.dot(contexts, w_out, preferred_element_type=jnp.float32)
        ).astype(jnp.bfloat16)
        return mid, rms_scale(mid.astype(jnp.float32), ffn_gain).astype(jnp.bfloat16)

    returned = []
    for local in range(local_count):
        pairs = pairs_in[:, local * CAP : (local + 1) * CAP].reshape(slots, -1)
        _, rows = rows_of(pairs, context_in[local].reshape(slots, -1))
        result = run_expert(rows, expert_in, expert_out, local, local_count)
        returned.append(exchange(result.reshape(devices, CAP, feat_dim)).reshape(slots, feat_dim))

    stream_mid = (
        embedded.astype(jnp.float32) + jnp.dot(context, w_out, preferred_element_type=jnp.float32)
    ).astype(jnp.bfloat16)
    ffn_input = rms_scale(stream_mid.astype(jnp.float32), ffn_gain).astype(jnp.bfloat16)
    affinity = jax.nn.sigmoid(jnp.dot(ffn_input, router_w, preferred_element_type=jnp.float32))
    chosen_hot = expert_ids[:, :, None] == jnp.arange(experts, dtype=jnp.int32)[None, None, :]
    picked = jnp.sum(jnp.where(chosen_hot, affinity[:, None, :], 0.0), axis=-1)
    route_weight = picked / jnp.sum(picked, axis=1, keepdims=True)

    mixed = stream_mid.astype(jnp.float32)
    for local in range(local_count):
        for route in range(2):
            hot = route_key[:, route][:, None] == row_keys[local][None, :]
            gathered = jnp.dot(
                hot.astype(jnp.bfloat16), returned[local], preferred_element_type=jnp.float32
            ).astype(jnp.bfloat16)
            mixed = mixed + route_weight[:, route : route + 1] * gathered.astype(jnp.float32)
    return mixed.astype(jnp.bfloat16)


def solution(mesh):
    placed = (
        P("tm", None),
        P(),
        P(),
        P(),
        P(),
        P(),
        P(),
        P(),
        P(),
        P(None, "tm", None),
        P("tm", None),
        P("tm", None),
        P("tm", None),
    )
    return jax.shard_map(
        shards, mesh=mesh, in_specs=placed, out_specs=P("tm", None), check_vma=False
    )
```

```python
import functools
import math

import jax
import jax.numpy as jnp
from jax import lax
from jax.experimental import pallas as pl
from jax.experimental.pallas import tpu as pltpu
from jax.sharding import PartitionSpec as P

HEAD_DIM = 128
WINDOW = 2048
CAP = 16

NORM_EPS = 1e-06
MASKED = -1e30


def from_behind(block, axis, distance):
    devices = range(lax.axis_size(axis))
    route = [(i - distance, i) for i in devices if i - distance in devices]
    return lax.ppermute(block, axis, route)


def rms_scale(values, gain_vec):
    mean_sq = jnp.mean(values * values, axis=-1, keepdims=True)
    return values * lax.rsqrt(mean_sq + NORM_EPS) * gain_vec


def head_norm(values):
    mean_sq = jnp.mean(values * values, axis=-1, keepdims=True)
    return values * lax.rsqrt(mean_sq + NORM_EPS)


def expert_body(steps, mid_ref, gain_ref, w_in_ref, w_out_ref, out_ref, rows_ref, total_ref):
    step = pl.program_id(1)

    @pl.when(step == 0)
    def _():
        mid = mid_ref[...].astype(jnp.float32)
        rows_ref[...] = rms_scale(mid, gain_ref[...]).astype(jnp.bfloat16)

    rows = rows_ref[...]
    nt = (((1,), (1,)), ((), ()))
    gate = lax.dot_general(rows, w_in_ref[0], nt, preferred_element_type=jnp.float32)
    up = lax.dot_general(rows, w_in_ref[1], nt, preferred_element_type=jnp.float32)
    hidden = (gate / (1.0 + jnp.exp(-gate)) * up).astype(jnp.bfloat16)
    part = jnp.dot(hidden, w_out_ref[...], preferred_element_type=jnp.float32)

    @pl.when(step == 0)
    def _():
        total_ref[...] = part

    @pl.when(step > 0)
    def _():
        total_ref[...] += part

    @pl.when(step == steps - 1)
    def _():
        out_ref[...] = total_ref[...].astype(out_ref.dtype)


def run_expert(mid, gain, expert_in, expert_out, local, local_count):
    row_total, feat_dim = mid.shape
    units = expert_out.shape[0] // local_count
    width = 352
    steps = units // width
    first = local * steps
    tile = math.gcd(row_total, 512)
    flops = 6 * row_total * units * feat_dim
    return pl.pallas_call(
        functools.partial(expert_body, steps),
        grid=(row_total // tile, steps),
        in_specs=[
            pl.BlockSpec((tile, feat_dim), lambda r, i: (r, 0)),
            pl.BlockSpec((1, feat_dim), lambda r, i: (0, 0)),
            pl.BlockSpec((2, width, feat_dim), lambda r, i: (0, first + i, 0)),
            pl.BlockSpec((width, feat_dim), lambda r, i: (first + i, 0)),
        ],
        out_specs=pl.BlockSpec((tile, feat_dim), lambda r, i: (r, 0)),
        out_shape=jax.ShapeDtypeStruct((row_total, feat_dim), jnp.bfloat16),
        scratch_shapes=[
            pltpu.VMEM((tile, feat_dim), jnp.bfloat16),
            pltpu.VMEM((tile, feat_dim), jnp.float32),
        ],
        compiler_params=pltpu.CompilerParams(vmem_limit_bytes=40 << 20),
        cost_estimate=pl.CostEstimate(
            flops=flops,
            bytes_accessed=6 * units * feat_dim + 4 * row_total * feat_dim,
            transcendentals=row_total * units,
        ),
    )(mid, gain.reshape(1, -1), expert_in, expert_out)


def kv_body(rows_ref, weight_ref, out_ref):
    both = jnp.dot(rows_ref[...], weight_ref[...], preferred_element_type=jnp.float32)
    kv_dim = both.shape[1] // 2
    for start in range(0, kv_dim, HEAD_DIM):
        head = both[:, start : start + HEAD_DIM]
        out_ref[:, start : start + HEAD_DIM] = head_norm(head).astype(out_ref.dtype)
    out_ref[:, kv_dim:] = both[:, kv_dim:].astype(out_ref.dtype)


def project_kv(rows, weight):
    row_count, feat_dim = rows.shape
    width = weight.shape[1]
    return pl.pallas_call(
        kv_body,
        out_shape=jax.ShapeDtypeStruct((row_count, width), jnp.bfloat16),
        in_specs=[pl.BlockSpec(memory_space=pltpu.VMEM)] * 2,
        out_specs=pl.BlockSpec(memory_space=pltpu.VMEM),
        compiler_params=pltpu.CompilerParams(vmem_limit_bytes=16 << 20),
        cost_estimate=pl.CostEstimate(
            flops=2 * row_count * feat_dim * width,
            bytes_accessed=2 * (row_count * feat_dim + feat_dim * width),
            transcendentals=row_count,
        ),
    )(rows, weight)


def attend_body(
    kv_heads, valid_ref, scale_ref, query_ref, *refs
):
    *kv_refs, out_ref, unit_ref, key_ref, value_ref, score_ref = refs
    blocks = [ref.at[part] for ref in kv_refs for part in range(ref.shape[0])]
    rows = query_ref.shape[0]
    heads = query_ref.shape[1] // HEAD_DIM
    group = heads // kv_heads
    kv_dim = kv_heads * HEAD_DIM
    for head in range(heads):
        unit_ref[head] = head_norm(
            query_ref[:, head * HEAD_DIM : (head + 1) * HEAD_DIM]
        ).astype(jnp.bfloat16)
    for pos, block in enumerate(blocks):
        for kv in range(kv_heads):
            low = kv * HEAD_DIM
            key_ref[kv, pos] = block[:, low : low + HEAD_DIM]
            value_ref[kv, pos, :, :HEAD_DIM] = block[:, kv_dim + low : kv_dim + low + HEAD_DIM]
            value_ref[kv, pos, :, HEAD_DIM:] = jnp.ones((rows, HEAD_DIM), jnp.bfloat16)
    query_at = lax.broadcasted_iota(jnp.int32, (rows, rows), 0)
    key_at = lax.broadcasted_iota(jnp.int32, (rows, rows), 1)

    @pl.loop(0, heads)
    def _(head):
        kv = head // group
        unit = unit_ref[head]
        top = jnp.full((rows, HEAD_DIM), MASKED, jnp.float32)
        for pos in range(len(blocks)):
            score = lax.dot_general(
                unit,
                key_ref[kv, pos],
                (((1,), (1,)), ((), ())),
                preferred_element_type=jnp.float32,
            )
            if pos == 0:
                score = jnp.where(key_at <= query_at, score, MASKED)
            else:
                seen = valid_ref[pos] > 0
                if pos == 1:
                    score = jnp.where((key_at > query_at) & seen, score, MASKED)
                else:
                    score = jnp.where(seen, score, MASKED)
            score_ref[pos] = score
            for low in range(0, rows, HEAD_DIM):
                top = jnp.maximum(top, score[:, low : low + HEAD_DIM])
        top = jnp.max(top, axis=1, keepdims=True)
        factor = scale_ref[head] * (math.log2(math.e) / math.sqrt(HEAD_DIM))
        total = jnp.zeros((rows, 2 * HEAD_DIM), jnp.float32)
        for pos in range(len(blocks)):
            weight = jnp.exp2((score_ref[pos] - top) * factor).astype(jnp.bfloat16)
            total += jnp.dot(weight, value_ref[kv, pos], preferred_element_type=jnp.float32)
        place = pl.ds(pl.multiple_of(head * HEAD_DIM, HEAD_DIM), HEAD_DIM)
        out_ref[:, place] = (total[:, :HEAD_DIM] / total[:, HEAD_DIM:]).astype(out_ref.dtype)


def attend(valid, head_scale, queries, kv_parts, kv_heads):
    rows, width = queries.shape
    heads = width // HEAD_DIM
    count = sum(part.shape[0] for part in kv_parts)
    smem = pl.BlockSpec(memory_space=pltpu.SMEM)
    vmem = pl.BlockSpec(memory_space=pltpu.VMEM)
    return pl.pallas_call(
        functools.partial(attend_body, kv_heads),
        out_shape=jax.ShapeDtypeStruct((rows, width), jnp.bfloat16),
        in_specs=[smem, smem, vmem] + [vmem] * len(kv_parts),
        out_specs=vmem,
        scratch_shapes=[
            pltpu.VMEM((heads, rows, HEAD_DIM), jnp.bfloat16),
            pltpu.VMEM((kv_heads, count, rows, HEAD_DIM), jnp.bfloat16),
            pltpu.VMEM((kv_heads, count, rows, 2 * HEAD_DIM), jnp.bfloat16),
            pltpu.VMEM((count, rows, rows), jnp.float32),
        ],
        compiler_params=pltpu.CompilerParams(vmem_limit_bytes=32 << 20),
        cost_estimate=pl.CostEstimate(
            flops=6 * heads * count * rows * rows * HEAD_DIM,
            bytes_accessed=rows * width * 6 + count * rows * kv_heads * HEAD_DIM * 4,
            transcendentals=heads * count * rows * rows,
        ),
    )(valid, head_scale, queries, *kv_parts)


def window_parts(own_kv, group):
    devices = lax.axis_size("tm")
    me = lax.axis_index("tm")
    core, chip, base = me % 2, me % group // 2, me // group * group
    prior = from_behind(own_kv, "tm", group)
    parts = [(own_kv, me), (prior, me - group)]
    fetched = []
    for step in range(1, group // 2):
        route = []
        for dev in range(devices):
            target = dev ^ (2 * step)
            target += 0 if dev < target else group
            if target < devices:
                route.append((dev, target))
        other = chip ^ step
        start = base - jnp.where(other > chip, group, 0) + 2 * other
        fetched.append((lax.ppermute(own_kv, "tm", route), start))
    shared = jnp.stack([block for block, _ in fetched] + [jnp.where(core == 0, own_kv, prior)])
    shared = lax.ppermute(shared, "tm", [(dev, dev ^ 1) for dev in range(devices)])
    numbers = [start + core for _, start in fetched]
    numbers += [start + 1 - core for _, start in fetched]
    numbers.append(jnp.where(core == 0, me + 1 - group, me - 1))
    blocks = [own_kv[None], prior[None]] + [block[None] for block, _ in fetched] + [shared]
    numbers = jnp.stack([me, me - group] + numbers)
    return blocks, numbers


def shards(
    signal,
    conv_weight,
    attn_gain,
    w_query,
    w_keyval,
    w_out,
    head_scale,
    ffn_gain,
    router_w,
    expert_in,
    expert_out,
    expert_ids,
    slot_ids,
):
    row_count = signal.shape[0]
    feat_dim = conv_weight.shape[1]
    devices = lax.axis_size("tm")
    dev_index = lax.axis_index("tm")
    experts = router_w.shape[1]
    copies = max(devices // experts, 1)
    local_count = max(experts // devices, 1)
    slots = devices * CAP

    route_key = expert_ids * CAP + slot_ids
    row_id = jnp.arange(slots, dtype=jnp.int32)
    row_dev, row_slot = row_id // CAP, row_id % CAP
    row_keys = [
        (row_dev // copies * local_count + local) * CAP + row_slot for local in range(local_count)
    ]

    def spread(values, local):
        hot = (row_keys[local][:, None] == route_key[None, :, 0]) | (
            row_keys[local][:, None] == route_key[None, :, 1]
        )
        return jnp.dot(
            hot.astype(jnp.bfloat16), values, preferred_element_type=jnp.float32
        ).astype(jnp.bfloat16)

    def exchange(rows):
        return lax.all_to_all(rows, "tm", split_axis=0, concat_axis=0, tiled=True)

    reach_blocks = WINDOW // row_count
    group = reach_blocks
    lines = devices // group
    before = from_behind(signal[row_count - 1 :], "tm", 1)
    previous = jnp.concatenate([before, signal[:-1]], axis=0)
    patch_pairs = jnp.concatenate([previous, signal], axis=1)

    ahead = jnp.concatenate(
        [
            signal,
            before,
            expert_ids.astype(jnp.bfloat16).T.reshape(-1, signal.shape[1]),
            slot_ids.astype(jnp.bfloat16).T.reshape(-1, signal.shape[1]),
        ],
        axis=0,
    )
    used = ahead.shape[0]
    ahead = jnp.pad(ahead, ((0, -used % 16), (0, 0)))
    line_groups = [[row * group + place for row in range(lines)] for place in range(group)]
    gathered = lax.all_gather(ahead, "tm", axis_index_groups=line_groups)

    embedded = jnp.dot(patch_pairs, conv_weight, preferred_element_type=jnp.float32).astype(
        jnp.bfloat16
    )
    normed = rms_scale(embedded.astype(jnp.float32), attn_gain).astype(jnp.bfloat16)
    kv_heads = w_keyval.shape[1] // 2 // HEAD_DIM
    own_kv = project_kv(normed, w_keyval)
    kv_parts, numbers = window_parts(own_kv, group)
    queries = jnp.dot(normed, w_query, preferred_element_type=jnp.float32)
    context = attend((numbers >= 0).astype(jnp.int32), head_scale, queries, kv_parts, kv_heads)

    line_signal = gathered[:, :row_count]
    line_before = gathered[:, row_count : row_count + 1]
    line_previous = jnp.concatenate([line_before, line_signal[:, :-1]], axis=1)
    line_pairs = jnp.concatenate([line_previous, line_signal], axis=2)
    id_rows = (used - row_count - 1) // 2
    line_ids = gathered[:, row_count + 1 : row_count + 1 + id_rows].astype(jnp.int32)
    line_slots = gathered[:, row_count + 1 + id_rows : used].astype(jnp.int32)
    line_keys = (line_ids * CAP + line_slots).reshape(lines, 2, 1, row_count)
    near_dev = dev_index // group * group + jnp.arange(group, dtype=jnp.int32)
    near_expert = (near_dev // copies * local_count)[:, None] + jnp.arange(
        local_count, dtype=jnp.int32
    )
    near_keys = near_expert[:, :, None] * CAP + jnp.arange(CAP, dtype=jnp.int32)
    near_keys = near_keys.reshape(1, -1, 1)
    line_hot = (near_keys == line_keys[:, 0]) | (near_keys == line_keys[:, 1])
    pairs_out = jnp.einsum(
        "lrt,ltf->rlf", line_hot.astype(jnp.bfloat16), line_pairs,
        preferred_element_type=jnp.float32,
    ).astype(jnp.bfloat16)
    pairs_out = pairs_out.reshape(group, local_count * CAP, lines, -1)
    near_groups = [[row * group + place for place in range(group)] for row in range(lines)]
    pairs_in = lax.all_to_all(
        pairs_out, "tm", split_axis=0, concat_axis=0, axis_index_groups=near_groups, tiled=True
    )
    pairs_in = pairs_in.transpose(2, 0, 1, 3).reshape(devices, local_count * CAP, -1)

    context_in = [
        exchange(spread(context, local).reshape(devices, CAP, -1)) for local in range(local_count)
    ]

    def mid_of(pairs, contexts):
        placed = jnp.dot(pairs, conv_weight, preferred_element_type=jnp.float32).astype(
            jnp.bfloat16
        )
        return (
            placed.astype(jnp.float32)
            + jnp.dot(contexts, w_out, preferred_element_type=jnp.float32)
        ).astype(jnp.bfloat16)

    returned = []
    for local in range(local_count):
        pairs = pairs_in[:, local * CAP : (local + 1) * CAP].reshape(slots, -1)
        contexts = context_in[local].reshape(slots, -1)
        mid = mid_of(pairs, contexts)
        result = run_expert(mid, ffn_gain, expert_in, expert_out, local, local_count)
        returned.append(exchange(result.reshape(devices, CAP, feat_dim)).reshape(slots, feat_dim))

    stream_mid = (
        embedded.astype(jnp.float32) + jnp.dot(context, w_out, preferred_element_type=jnp.float32)
    ).astype(jnp.bfloat16)
    ffn_input = rms_scale(stream_mid.astype(jnp.float32), ffn_gain).astype(jnp.bfloat16)
    affinity = jax.nn.sigmoid(jnp.dot(ffn_input, router_w, preferred_element_type=jnp.float32))
    chosen_hot = expert_ids[:, :, None] == jnp.arange(experts, dtype=jnp.int32)[None, None, :]
    picked = jnp.sum(jnp.where(chosen_hot, affinity[:, None, :], 0.0), axis=-1)
    route_weight = picked / jnp.sum(picked, axis=1, keepdims=True)

    mixed = stream_mid.astype(jnp.float32)
    for local in range(local_count):
        for route in range(2):
            hot = route_key[:, route][:, None] == row_keys[local][None, :]
            gathered = jnp.dot(
                hot.astype(jnp.bfloat16), returned[local], preferred_element_type=jnp.float32
            ).astype(jnp.bfloat16)
            mixed = mixed + route_weight[:, route : route + 1] * gathered.astype(jnp.float32)
    return mixed.astype(jnp.bfloat16)


def solution(mesh):
    placed = (
        P("tm", None),
        P(),
        P(),
        P(),
        P(),
        P(),
        P(),
        P(),
        P(),
        P(None, "tm", None),
        P("tm", None),
        P("tm", None),
        P("tm", None),
    )
    return jax.shard_map(
        shards, mesh=mesh, in_specs=placed, out_specs=P("tm", None), check_vma=False
    )
```

```python
import functools
import math

import jax
import jax.numpy as jnp
from jax import lax
from jax.experimental import pallas as pl
from jax.experimental.pallas import tpu as pltpu
from jax.sharding import PartitionSpec as P

HEAD_DIM = 128
WINDOW = 2048
CAP = 16

NORM_EPS = 1e-06
MASKED = -1e30


def from_behind(block, axis, distance):
    devices = range(lax.axis_size(axis))
    route = [(i - distance, i) for i in devices if i - distance in devices]
    return lax.ppermute(block, axis, route)


def rms_scale(values, gain_vec):
    mean_sq = jnp.mean(values * values, axis=-1, keepdims=True)
    return values * lax.rsqrt(mean_sq + NORM_EPS) * gain_vec


def head_norm(values):
    mean_sq = jnp.mean(values * values, axis=-1, keepdims=True)
    return values * lax.rsqrt(mean_sq + NORM_EPS)


def expert_body(steps, mid_ref, gain_ref, w_in_ref, w_out_ref, out_ref, rows_ref, total_ref):
    step = pl.program_id(1)

    @pl.when(step == 0)
    def _():
        mid = mid_ref[...].astype(jnp.float32)
        rows_ref[...] = rms_scale(mid, gain_ref[...]).astype(jnp.bfloat16)

    rows = rows_ref[...]
    nt = (((1,), (1,)), ((), ()))
    gate = lax.dot_general(rows, w_in_ref[0], nt, preferred_element_type=jnp.float32)
    up = lax.dot_general(rows, w_in_ref[1], nt, preferred_element_type=jnp.float32)
    hidden = (gate / (1.0 + jnp.exp(-gate)) * up).astype(jnp.bfloat16)
    part = jnp.dot(hidden, w_out_ref[...], preferred_element_type=jnp.float32)

    @pl.when(step == 0)
    def _():
        total_ref[...] = part

    @pl.when(step > 0)
    def _():
        total_ref[...] += part

    @pl.when(step == steps - 1)
    def _():
        out_ref[...] = total_ref[...].astype(out_ref.dtype)


def run_expert(mid, gain, expert_in, expert_out, local, local_count):
    row_total, feat_dim = mid.shape
    units = expert_out.shape[0] // local_count
    width = 352
    steps = units // width
    first = local * steps
    tile = math.gcd(row_total, 512)
    flops = 6 * row_total * units * feat_dim
    return pl.pallas_call(
        functools.partial(expert_body, steps),
        grid=(row_total // tile, steps),
        in_specs=[
            pl.BlockSpec((tile, feat_dim), lambda r, i: (r, 0)),
            pl.BlockSpec((1, feat_dim), lambda r, i: (0, 0)),
            pl.BlockSpec((2, width, feat_dim), lambda r, i: (0, first + i, 0)),
            pl.BlockSpec((width, feat_dim), lambda r, i: (first + i, 0)),
        ],
        out_specs=pl.BlockSpec((tile, feat_dim), lambda r, i: (r, 0)),
        out_shape=jax.ShapeDtypeStruct((row_total, feat_dim), jnp.bfloat16),
        scratch_shapes=[
            pltpu.VMEM((tile, feat_dim), jnp.bfloat16),
            pltpu.VMEM((tile, feat_dim), jnp.float32),
        ],
        compiler_params=pltpu.CompilerParams(vmem_limit_bytes=40 << 20),
        cost_estimate=pl.CostEstimate(
            flops=flops,
            bytes_accessed=6 * units * feat_dim + 4 * row_total * feat_dim,
            transcendentals=row_total * units,
        ),
    )(mid, gain.reshape(1, -1), expert_in, expert_out)


def kv_body(rows_ref, weight_ref, out_ref):
    both = jnp.dot(rows_ref[...], weight_ref[...], preferred_element_type=jnp.float32)
    kv_dim = both.shape[1] // 2
    for start in range(0, kv_dim, HEAD_DIM):
        head = both[:, start : start + HEAD_DIM]
        out_ref[:, start : start + HEAD_DIM] = head_norm(head).astype(out_ref.dtype)
    out_ref[:, kv_dim:] = both[:, kv_dim:].astype(out_ref.dtype)


def project_kv(rows, weight):
    row_count, feat_dim = rows.shape
    width = weight.shape[1]
    return pl.pallas_call(
        kv_body,
        out_shape=jax.ShapeDtypeStruct((row_count, width), jnp.bfloat16),
        in_specs=[pl.BlockSpec(memory_space=pltpu.VMEM)] * 2,
        out_specs=pl.BlockSpec(memory_space=pltpu.VMEM),
        compiler_params=pltpu.CompilerParams(vmem_limit_bytes=16 << 20),
        cost_estimate=pl.CostEstimate(
            flops=2 * row_count * feat_dim * width,
            bytes_accessed=2 * (row_count * feat_dim + feat_dim * width),
            transcendentals=row_count,
        ),
    )(rows, weight)


def attend_body(
    kv_heads, valid_ref, scale_ref, query_ref, *refs
):
    *kv_refs, out_ref, unit_ref, key_ref, value_ref, score_ref = refs
    blocks = [ref.at[part] for ref in kv_refs for part in range(ref.shape[0])]
    rows = query_ref.shape[0]
    heads = query_ref.shape[1] // HEAD_DIM
    group = heads // kv_heads
    kv_dim = kv_heads * HEAD_DIM
    for head in range(heads):
        unit_ref[head] = head_norm(
            query_ref[:, head * HEAD_DIM : (head + 1) * HEAD_DIM]
        ).astype(jnp.bfloat16)
    for pos, block in enumerate(blocks):
        for kv in range(kv_heads):
            low = kv * HEAD_DIM
            key_ref[kv, pos] = block[:, low : low + HEAD_DIM]
            value_ref[kv, pos, :, :HEAD_DIM] = block[:, kv_dim + low : kv_dim + low + HEAD_DIM]
            value_ref[kv, pos, :, HEAD_DIM:] = jnp.ones((rows, HEAD_DIM), jnp.bfloat16)
    query_at = lax.broadcasted_iota(jnp.int32, (rows, rows), 0)
    key_at = lax.broadcasted_iota(jnp.int32, (rows, rows), 1)

    @pl.loop(0, heads)
    def _(head):
        kv = head // group
        unit = unit_ref[head]
        top = jnp.full((rows, HEAD_DIM), MASKED, jnp.float32)
        for pos in range(len(blocks)):
            score = lax.dot_general(
                unit,
                key_ref[kv, pos],
                (((1,), (1,)), ((), ())),
                preferred_element_type=jnp.float32,
            )
            if pos == 0:
                score = jnp.where(key_at <= query_at, score, MASKED)
            else:
                seen = valid_ref[pos] > 0
                if pos == 1:
                    score = jnp.where((key_at > query_at) & seen, score, MASKED)
                else:
                    score = jnp.where(seen, score, MASKED)
            score_ref[pos] = score
            for low in range(0, rows, HEAD_DIM):
                top = jnp.maximum(top, score[:, low : low + HEAD_DIM])
        top = jnp.max(top, axis=1, keepdims=True)
        factor = scale_ref[head] * (math.log2(math.e) / math.sqrt(HEAD_DIM))
        total = jnp.zeros((rows, 2 * HEAD_DIM), jnp.float32)
        for pos in range(len(blocks)):
            weight = jnp.exp2((score_ref[pos] - top) * factor).astype(jnp.bfloat16)
            total += jnp.dot(weight, value_ref[kv, pos], preferred_element_type=jnp.float32)
        place = pl.ds(pl.multiple_of(head * HEAD_DIM, HEAD_DIM), HEAD_DIM)
        out_ref[:, place] = (total[:, :HEAD_DIM] / total[:, HEAD_DIM:]).astype(out_ref.dtype)


def attend(valid, head_scale, queries, kv_parts, kv_heads):
    rows, width = queries.shape
    heads = width // HEAD_DIM
    count = sum(part.shape[0] for part in kv_parts)
    smem = pl.BlockSpec(memory_space=pltpu.SMEM)
    vmem = pl.BlockSpec(memory_space=pltpu.VMEM)
    return pl.pallas_call(
        functools.partial(attend_body, kv_heads),
        out_shape=jax.ShapeDtypeStruct((rows, width), jnp.bfloat16),
        in_specs=[smem, smem, vmem] + [vmem] * len(kv_parts),
        out_specs=vmem,
        scratch_shapes=[
            pltpu.VMEM((heads, rows, HEAD_DIM), jnp.bfloat16),
            pltpu.VMEM((kv_heads, count, rows, HEAD_DIM), jnp.bfloat16),
            pltpu.VMEM((kv_heads, count, rows, 2 * HEAD_DIM), jnp.bfloat16),
            pltpu.VMEM((count, rows, rows), jnp.float32),
        ],
        compiler_params=pltpu.CompilerParams(vmem_limit_bytes=32 << 20),
        cost_estimate=pl.CostEstimate(
            flops=6 * heads * count * rows * rows * HEAD_DIM,
            bytes_accessed=rows * width * 6 + count * rows * kv_heads * HEAD_DIM * 4,
            transcendentals=heads * count * rows * rows,
        ),
    )(valid, head_scale, queries, *kv_parts)


def window_parts(own_kv, group):
    devices = lax.axis_size("tm")
    me = lax.axis_index("tm")
    core, chip, base = me % 2, me % group // 2, me // group * group
    prior = from_behind(own_kv, "tm", group)
    parts = [(own_kv, me), (prior, me - group)]
    fetched = []
    for step in range(1, group // 2):
        route = []
        for dev in range(devices):
            target = dev ^ (2 * step)
            target += 0 if dev < target else group
            if target < devices:
                route.append((dev, target))
        other = chip ^ step
        start = base - jnp.where(other > chip, group, 0) + 2 * other
        fetched.append((lax.ppermute(own_kv, "tm", route), start))
    shared = jnp.stack([block for block, _ in fetched] + [jnp.where(core == 0, own_kv, prior)])
    shared = lax.ppermute(shared, "tm", [(dev, dev ^ 1) for dev in range(devices)])
    numbers = [start + core for _, start in fetched]
    numbers += [start + 1 - core for _, start in fetched]
    numbers.append(jnp.where(core == 0, me + 1 - group, me - 1))
    blocks = [own_kv[None], prior[None]] + [block[None] for block, _ in fetched] + [shared]
    numbers = jnp.stack([me, me - group] + numbers)
    return blocks, numbers


def shards(
    signal,
    conv_weight,
    attn_gain,
    w_query,
    w_keyval,
    w_out,
    head_scale,
    ffn_gain,
    router_w,
    expert_in,
    expert_out,
    expert_ids,
    slot_ids,
):
    row_count = signal.shape[0]
    feat_dim = conv_weight.shape[1]
    devices = lax.axis_size("tm")
    dev_index = lax.axis_index("tm")
    experts = router_w.shape[1]
    copies = max(devices // experts, 1)
    local_count = max(experts // devices, 1)
    slots = devices * CAP

    route_key = expert_ids * CAP + slot_ids
    row_id = jnp.arange(slots, dtype=jnp.int32)
    row_dev, row_slot = row_id // CAP, row_id % CAP
    row_keys = [
        (row_dev // copies * local_count + local) * CAP + row_slot for local in range(local_count)
    ]

    def spread(values, local):
        hot = (row_keys[local][:, None] == route_key[None, :, 0]) | (
            row_keys[local][:, None] == route_key[None, :, 1]
        )
        return jnp.dot(
            hot.astype(jnp.bfloat16), values, preferred_element_type=jnp.float32
        ).astype(jnp.bfloat16)

    def exchange(rows):
        return lax.all_to_all(rows, "tm", split_axis=0, concat_axis=0, tiled=True)

    reach_blocks = WINDOW // row_count
    group = reach_blocks
    before = from_behind(signal[row_count - 1 :], "tm", 1)
    previous = jnp.concatenate([before, signal[:-1]], axis=0)
    patch_pairs = jnp.concatenate([previous, signal], axis=1)

    ahead = jnp.concatenate(
        [
            signal,
            before,
            expert_ids.astype(jnp.bfloat16).T.reshape(-1, signal.shape[1]),
            slot_ids.astype(jnp.bfloat16).T.reshape(-1, signal.shape[1]),
        ],
        axis=0,
    )
    used = ahead.shape[0]
    ahead = jnp.pad(ahead, ((0, -used % 16), (0, 0)))
    half = devices // 2
    far = lax.ppermute(ahead, "tm", [(dev, (dev + half) % devices) for dev in range(devices)])

    embedded = jnp.dot(patch_pairs, conv_weight, preferred_element_type=jnp.float32).astype(
        jnp.bfloat16
    )
    normed = rms_scale(embedded.astype(jnp.float32), attn_gain).astype(jnp.bfloat16)
    kv_heads = w_keyval.shape[1] // 2 // HEAD_DIM
    own_kv = project_kv(normed, w_keyval)
    kv_parts, numbers = window_parts(own_kv, group)
    queries = jnp.dot(normed, w_query, preferred_element_type=jnp.float32)
    context = attend((numbers >= 0).astype(jnp.int32), head_scale, queries, kv_parts, kv_heads)

    far, _ = lax.optimization_barrier((far, own_kv))
    in_first = dev_index < half
    both = jnp.stack([jnp.where(in_first, ahead, far), jnp.where(in_first, far, ahead)])
    both_signal = both[:, :row_count]
    both_before = both[:, row_count : row_count + 1]
    both_previous = jnp.concatenate([both_before, both_signal[:, :-1]], axis=1)
    both_pairs = jnp.concatenate([both_previous, both_signal], axis=2)
    both_pairs = both_pairs.reshape(2 * row_count, -1)
    id_rows = (used - row_count - 1) // 2
    both_ids = both[:, row_count + 1 : row_count + 1 + id_rows].astype(jnp.int32)
    both_slots = both[:, row_count + 1 + id_rows : used].astype(jnp.int32)
    both_keys = (both_ids * CAP + both_slots).reshape(2, 2, row_count)
    span = experts * CAP
    both_keys = both_keys + span * jnp.arange(2, dtype=jnp.int32)[:, None, None]
    both_keys = both_keys.transpose(1, 0, 2).reshape(2, 1, 2 * row_count)
    place = jnp.arange(half * 2 * local_count * CAP, dtype=jnp.int32)
    place_slot = place % CAP
    place_local = place // CAP % local_count
    place_block = place // (CAP * local_count) % 2
    place_dev = place // (CAP * local_count * 2) + jnp.where(in_first, 0, half)
    place_key = (place_dev // copies * local_count + place_local) * CAP + place_slot
    place_key = (place_key + span * place_block)[:, None]
    both_hot = (place_key == both_keys[0]) | (place_key == both_keys[1])
    pairs_out = jnp.dot(
        both_hot.astype(jnp.bfloat16), both_pairs, preferred_element_type=jnp.float32
    ).astype(jnp.bfloat16)
    pairs_out, _ = lax.optimization_barrier((pairs_out, kv_parts[1:-1]))
    pairs_in = lax.all_to_all(
        pairs_out.reshape(half, 2 * local_count * CAP, -1),
        "tm",
        split_axis=0,
        concat_axis=0,
        axis_index_groups=[list(range(half)), list(range(half, devices))],
        tiled=True,
    )
    pairs_in = pairs_in.reshape(half, 2, local_count, CAP, -1)

    context_in = [
        exchange(spread(context, local).reshape(devices, CAP, -1)) for local in range(local_count)
    ]

    def mid_of(pairs, contexts):
        placed = jnp.dot(pairs, conv_weight, preferred_element_type=jnp.float32).astype(
            jnp.bfloat16
        )
        return (
            placed.astype(jnp.float32)
            + jnp.dot(contexts, w_out, preferred_element_type=jnp.float32)
        ).astype(jnp.bfloat16)

    returned = []
    for local in range(local_count):
        pairs = pairs_in[:, :, local].transpose(1, 0, 2, 3).reshape(slots, -1)
        contexts = context_in[local].reshape(slots, -1)
        mid = mid_of(pairs, contexts)
        result = run_expert(mid, ffn_gain, expert_in, expert_out, local, local_count)
        returned.append(exchange(result.reshape(devices, CAP, feat_dim)).reshape(slots, feat_dim))

    stream_mid = (
        embedded.astype(jnp.float32) + jnp.dot(context, w_out, preferred_element_type=jnp.float32)
    ).astype(jnp.bfloat16)
    ffn_input = rms_scale(stream_mid.astype(jnp.float32), ffn_gain).astype(jnp.bfloat16)
    affinity = jax.nn.sigmoid(jnp.dot(ffn_input, router_w, preferred_element_type=jnp.float32))
    chosen_hot = expert_ids[:, :, None] == jnp.arange(experts, dtype=jnp.int32)[None, None, :]
    picked = jnp.sum(jnp.where(chosen_hot, affinity[:, None, :], 0.0), axis=-1)
    route_weight = picked / jnp.sum(picked, axis=1, keepdims=True)

    mixed = stream_mid.astype(jnp.float32)
    for local in range(local_count):
        for route in range(2):
            hot = route_key[:, route][:, None] == row_keys[local][None, :]
            gathered = jnp.dot(
                hot.astype(jnp.bfloat16), returned[local], preferred_element_type=jnp.float32
            ).astype(jnp.bfloat16)
            mixed = mixed + route_weight[:, route : route + 1] * gathered.astype(jnp.float32)
    return mixed.astype(jnp.bfloat16)


def solution(mesh):
    placed = (
        P("tm", None),
        P(),
        P(),
        P(),
        P(),
        P(),
        P(),
        P(),
        P(),
        P(None, "tm", None),
        P("tm", None),
        P("tm", None),
        P("tm", None),
    )
    return jax.shard_map(
        shards, mesh=mesh, in_specs=placed, out_specs=P("tm", None), check_vma=False
    )
```

```python
import functools
import math

import jax
import jax.numpy as jnp
from jax import lax
from jax.experimental import pallas as pl
from jax.experimental.pallas import tpu as pltpu
from jax.sharding import PartitionSpec as P

HEAD_DIM = 128
WINDOW = 2048
CAP = 16

NORM_EPS = 1e-06
MASKED = -1e30


def from_behind(block, axis, distance):
    devices = range(lax.axis_size(axis))
    route = [(i - distance, i) for i in devices if i - distance in devices]
    return lax.ppermute(block, axis, route)


def rms_scale(values, gain_vec):
    mean_sq = jnp.mean(values * values, axis=-1, keepdims=True)
    return values * lax.rsqrt(mean_sq + NORM_EPS) * gain_vec


def head_norm(values):
    mean_sq = jnp.mean(values * values, axis=-1, keepdims=True)
    return values * lax.rsqrt(mean_sq + NORM_EPS)


def expert_body(steps, mid_ref, gain_ref, w_in_ref, w_out_ref, out_ref, rows_ref, total_ref):
    step = pl.program_id(1)

    @pl.when(step == 0)
    def _():
        mid = mid_ref[...].astype(jnp.float32)
        rows_ref[...] = rms_scale(mid, gain_ref[...]).astype(jnp.bfloat16)

    rows = rows_ref[...]
    nt = (((1,), (1,)), ((), ()))
    gate = lax.dot_general(rows, w_in_ref[0], nt, preferred_element_type=jnp.float32)
    up = lax.dot_general(rows, w_in_ref[1], nt, preferred_element_type=jnp.float32)
    hidden = (gate / (1.0 + jnp.exp(-gate)) * up).astype(jnp.bfloat16)
    part = jnp.dot(hidden, w_out_ref[...], preferred_element_type=jnp.float32)

    @pl.when(step == 0)
    def _():
        total_ref[...] = part

    @pl.when(step > 0)
    def _():
        total_ref[...] += part

    @pl.when(step == steps - 1)
    def _():
        out_ref[...] = total_ref[...].astype(out_ref.dtype)


def run_expert(mid, gain, expert_in, expert_out, local, local_count):
    row_total, feat_dim = mid.shape
    units = expert_out.shape[0] // local_count
    width = 352
    steps = units // width
    first = local * steps
    tile = math.gcd(row_total, 512)
    flops = 6 * row_total * units * feat_dim
    return pl.pallas_call(
        functools.partial(expert_body, steps),
        grid=(row_total // tile, steps),
        in_specs=[
            pl.BlockSpec((tile, feat_dim), lambda r, i: (r, 0)),
            pl.BlockSpec((1, feat_dim), lambda r, i: (0, 0)),
            pl.BlockSpec((2, width, feat_dim), lambda r, i: (0, first + i, 0)),
            pl.BlockSpec((width, feat_dim), lambda r, i: (first + i, 0)),
        ],
        out_specs=pl.BlockSpec((tile, feat_dim), lambda r, i: (r, 0)),
        out_shape=jax.ShapeDtypeStruct((row_total, feat_dim), jnp.bfloat16),
        scratch_shapes=[
            pltpu.VMEM((tile, feat_dim), jnp.bfloat16),
            pltpu.VMEM((tile, feat_dim), jnp.float32),
        ],
        compiler_params=pltpu.CompilerParams(vmem_limit_bytes=40 << 20),
        cost_estimate=pl.CostEstimate(
            flops=flops,
            bytes_accessed=6 * units * feat_dim + 4 * row_total * feat_dim,
            transcendentals=row_total * units,
        ),
    )(mid, gain.reshape(1, -1), expert_in, expert_out)


def combine_body(base_ref, weight_ref, key_ref, row_ref, rows_ref, out_ref):
    total = base_ref[...]
    for route in range(2):
        hot = (key_ref[:, route : route + 1] == row_ref[...]).astype(jnp.bfloat16)
        rows = jnp.dot(hot, rows_ref[...], preferred_element_type=jnp.float32)
        rows = rows.astype(jnp.bfloat16).astype(jnp.float32)
        total = total + weight_ref[:, route : route + 1] * rows
    out_ref[...] = total.astype(out_ref.dtype)


def combine(base, weight, key, row_key, rows, kind):
    row_count, feat_dim = base.shape
    slots = rows.shape[0]
    width = math.gcd(feat_dim, 512)
    return pl.pallas_call(
        combine_body,
        grid=(feat_dim // width,),
        in_specs=[
            pl.BlockSpec((row_count, width), lambda i: (0, i)),
            pl.BlockSpec((row_count, 2), lambda i: (0, 0)),
            pl.BlockSpec((row_count, 2), lambda i: (0, 0)),
            pl.BlockSpec((1, slots), lambda i: (0, 0)),
            pl.BlockSpec((slots, width), lambda i: (0, i)),
        ],
        out_specs=pl.BlockSpec((row_count, width), lambda i: (0, i)),
        out_shape=jax.ShapeDtypeStruct((row_count, feat_dim), kind),
        compiler_params=pltpu.CompilerParams(vmem_limit_bytes=24 << 20),
        cost_estimate=pl.CostEstimate(
            flops=4 * row_count * slots * feat_dim,
            bytes_accessed=2 * slots * feat_dim + 8 * row_count * feat_dim,
            transcendentals=0,
        ),
    )(base, weight, key, row_key.reshape(1, -1), rows)


def kv_body(rows_ref, weight_ref, out_ref):
    both = jnp.dot(rows_ref[...], weight_ref[...], preferred_element_type=jnp.float32)
    kv_dim = both.shape[1] // 2
    for start in range(0, kv_dim, HEAD_DIM):
        head = both[:, start : start + HEAD_DIM]
        out_ref[:, start : start + HEAD_DIM] = head_norm(head).astype(out_ref.dtype)
    out_ref[:, kv_dim:] = both[:, kv_dim:].astype(out_ref.dtype)


def project_kv(rows, weight):
    row_count, feat_dim = rows.shape
    width = weight.shape[1]
    return pl.pallas_call(
        kv_body,
        out_shape=jax.ShapeDtypeStruct((row_count, width), jnp.bfloat16),
        in_specs=[pl.BlockSpec(memory_space=pltpu.VMEM)] * 2,
        out_specs=pl.BlockSpec(memory_space=pltpu.VMEM),
        compiler_params=pltpu.CompilerParams(vmem_limit_bytes=16 << 20),
        cost_estimate=pl.CostEstimate(
            flops=2 * row_count * feat_dim * width,
            bytes_accessed=2 * (row_count * feat_dim + feat_dim * width),
            transcendentals=row_count,
        ),
    )(rows, weight)


def attend_body(
    kv_heads, valid_ref, scale_ref, query_ref, *refs
):
    *kv_refs, out_ref, unit_ref, key_ref, value_ref, score_ref = refs
    blocks = [ref.at[part] for ref in kv_refs for part in range(ref.shape[0])]
    rows = query_ref.shape[0]
    heads = query_ref.shape[1] // HEAD_DIM
    group = heads // kv_heads
    kv_dim = kv_heads * HEAD_DIM
    for head in range(heads):
        unit_ref[head] = head_norm(
            query_ref[:, head * HEAD_DIM : (head + 1) * HEAD_DIM]
        ).astype(jnp.bfloat16)
    for pos, block in enumerate(blocks):
        for kv in range(kv_heads):
            low = kv * HEAD_DIM
            key_ref[kv, pos] = block[:, low : low + HEAD_DIM]
            value_ref[kv, pos, :, :HEAD_DIM] = block[:, kv_dim + low : kv_dim + low + HEAD_DIM]
            value_ref[kv, pos, :, HEAD_DIM:] = jnp.ones((rows, HEAD_DIM), jnp.bfloat16)
    query_at = lax.broadcasted_iota(jnp.int32, (rows, rows), 0)
    key_at = lax.broadcasted_iota(jnp.int32, (rows, rows), 1)

    @pl.loop(0, heads)
    def _(head):
        kv = head // group
        unit = unit_ref[head]
        top = jnp.full((rows, HEAD_DIM), MASKED, jnp.float32)
        for pos in range(len(blocks)):
            score = lax.dot_general(
                unit,
                key_ref[kv, pos],
                (((1,), (1,)), ((), ())),
                preferred_element_type=jnp.float32,
            )
            if pos == 0:
                score = jnp.where(key_at <= query_at, score, MASKED)
            else:
                seen = valid_ref[pos] > 0
                if pos == 1:
                    score = jnp.where((key_at > query_at) & seen, score, MASKED)
                else:
                    score = jnp.where(seen, score, MASKED)
            score_ref[pos] = score
            for low in range(0, rows, HEAD_DIM):
                top = jnp.maximum(top, score[:, low : low + HEAD_DIM])
        top = jnp.max(top, axis=1, keepdims=True)
        factor = scale_ref[head] * (math.log2(math.e) / math.sqrt(HEAD_DIM))
        total = jnp.zeros((rows, 2 * HEAD_DIM), jnp.float32)
        for pos in range(len(blocks)):
            weight = jnp.exp2((score_ref[pos] - top) * factor).astype(jnp.bfloat16)
            total += jnp.dot(weight, value_ref[kv, pos], preferred_element_type=jnp.float32)
        place = pl.ds(pl.multiple_of(head * HEAD_DIM, HEAD_DIM), HEAD_DIM)
        out_ref[:, place] = (total[:, :HEAD_DIM] / total[:, HEAD_DIM:]).astype(out_ref.dtype)


def attend(valid, head_scale, queries, kv_parts, kv_heads):
    rows, width = queries.shape
    heads = width // HEAD_DIM
    count = sum(part.shape[0] for part in kv_parts)
    smem = pl.BlockSpec(memory_space=pltpu.SMEM)
    vmem = pl.BlockSpec(memory_space=pltpu.VMEM)
    return pl.pallas_call(
        functools.partial(attend_body, kv_heads),
        out_shape=jax.ShapeDtypeStruct((rows, width), jnp.bfloat16),
        in_specs=[smem, smem, vmem] + [vmem] * len(kv_parts),
        out_specs=vmem,
        scratch_shapes=[
            pltpu.VMEM((heads, rows, HEAD_DIM), jnp.bfloat16),
            pltpu.VMEM((kv_heads, count, rows, HEAD_DIM), jnp.bfloat16),
            pltpu.VMEM((kv_heads, count, rows, 2 * HEAD_DIM), jnp.bfloat16),
            pltpu.VMEM((count, rows, rows), jnp.float32),
        ],
        compiler_params=pltpu.CompilerParams(vmem_limit_bytes=32 << 20),
        cost_estimate=pl.CostEstimate(
            flops=6 * heads * count * rows * rows * HEAD_DIM,
            bytes_accessed=rows * width * 6 + count * rows * kv_heads * HEAD_DIM * 4,
            transcendentals=heads * count * rows * rows,
        ),
    )(valid, head_scale, queries, *kv_parts)


def window_parts(own_kv, group):
    devices = lax.axis_size("tm")
    me = lax.axis_index("tm")
    core, chip, base = me % 2, me % group // 2, me // group * group
    prior = from_behind(own_kv, "tm", group)
    parts = [(own_kv, me), (prior, me - group)]
    fetched = []
    for step in range(1, group // 2):
        route = []
        for dev in range(devices):
            target = dev ^ (2 * step)
            target += 0 if dev < target else group
            if target < devices:
                route.append((dev, target))
        other = chip ^ step
        start = base - jnp.where(other > chip, group, 0) + 2 * other
        fetched.append((lax.ppermute(own_kv, "tm", route), start))
    shared = jnp.stack([block for block, _ in fetched] + [jnp.where(core == 0, own_kv, prior)])
    shared = lax.ppermute(shared, "tm", [(dev, dev ^ 1) for dev in range(devices)])
    numbers = [start + core for _, start in fetched]
    numbers += [start + 1 - core for _, start in fetched]
    numbers.append(jnp.where(core == 0, me + 1 - group, me - 1))
    blocks = [own_kv[None], prior[None]] + [block[None] for block, _ in fetched] + [shared]
    numbers = jnp.stack([me, me - group] + numbers)
    return blocks, numbers


def shards(
    signal,
    conv_weight,
    attn_gain,
    w_query,
    w_keyval,
    w_out,
    head_scale,
    ffn_gain,
    router_w,
    expert_in,
    expert_out,
    expert_ids,
    slot_ids,
):
    row_count = signal.shape[0]
    feat_dim = conv_weight.shape[1]
    devices = lax.axis_size("tm")
    dev_index = lax.axis_index("tm")
    experts = router_w.shape[1]
    copies = max(devices // experts, 1)
    local_count = max(experts // devices, 1)
    slots = devices * CAP

    route_key = expert_ids * CAP + slot_ids
    row_id = jnp.arange(slots, dtype=jnp.int32)
    row_dev, row_slot = row_id // CAP, row_id % CAP
    row_keys = [
        (row_dev // copies * local_count + local) * CAP + row_slot for local in range(local_count)
    ]

    def spread(values, local):
        hot = (row_keys[local][:, None] == route_key[None, :, 0]) | (
            row_keys[local][:, None] == route_key[None, :, 1]
        )
        return jnp.dot(
            hot.astype(jnp.bfloat16), values, preferred_element_type=jnp.float32
        ).astype(jnp.bfloat16)

    def exchange(rows):
        return lax.all_to_all(rows, "tm", split_axis=0, concat_axis=0, tiled=True)

    reach_blocks = WINDOW // row_count
    group = reach_blocks
    before = from_behind(signal[row_count - 1 :], "tm", 1)
    previous = jnp.concatenate([before, signal[:-1]], axis=0)
    patch_pairs = jnp.concatenate([previous, signal], axis=1)

    half = devices // 2
    routes = [
        table.astype(jnp.bfloat16).T.reshape(-1, signal.shape[1]) for table in (expert_ids, slot_ids)
    ]
    used = row_count + 2 * routes[0].shape[0]
    ahead = jnp.concatenate([signal] + routes, axis=0)
    ahead = jnp.pad(ahead, ((0, -used % 16), (0, 0)))
    far = lax.ppermute(ahead, "tm", [(dev, (dev + half) % devices) for dev in range(devices)])
    far_before = lax.ppermute(
        signal[row_count - 1 :],
        "tm",
        [(dev, (dev + 1 + half) % devices) for dev in range(devices - 1)],
    )

    embedded = jnp.dot(patch_pairs, conv_weight, preferred_element_type=jnp.float32).astype(
        jnp.bfloat16
    )
    normed = rms_scale(embedded.astype(jnp.float32), attn_gain).astype(jnp.bfloat16)
    kv_heads = w_keyval.shape[1] // 2 // HEAD_DIM
    own_kv = project_kv(normed, w_keyval)
    kv_parts, numbers = window_parts(own_kv, group)
    queries = jnp.dot(normed, w_query, preferred_element_type=jnp.float32)
    context = attend((numbers >= 0).astype(jnp.int32), head_scale, queries, kv_parts, kv_heads)

    far, _ = lax.optimization_barrier((far, own_kv))
    in_first = dev_index < half
    far_signal = far[:row_count]
    far_previous = jnp.concatenate([far_before, far_signal[:-1]], axis=0)
    far_pairs = jnp.concatenate([far_previous, far_signal], axis=1)
    both_pairs = jnp.concatenate(
        [jnp.where(in_first, patch_pairs, far_pairs), jnp.where(in_first, far_pairs, patch_pairs)]
    )
    far_tables = far[row_count:used].astype(jnp.int32).reshape(2, 2, row_count)
    far_key = far_tables[0] * CAP + far_tables[1]
    own_key = route_key.T
    both_keys = jnp.stack(
        [jnp.where(in_first, own_key, far_key), jnp.where(in_first, far_key, own_key)]
    )
    span = experts * CAP
    both_keys = both_keys + span * jnp.arange(2, dtype=jnp.int32)[:, None, None]
    both_keys = both_keys.transpose(1, 0, 2).reshape(2, 1, 2 * row_count)
    place = jnp.arange(half * 2 * local_count * CAP, dtype=jnp.int32)
    place_slot = place % CAP
    place_local = place // CAP % local_count
    place_block = place // (CAP * local_count) % 2
    place_dev = place // (CAP * local_count * 2) + jnp.where(in_first, 0, half)
    place_key = (place_dev // copies * local_count + place_local) * CAP + place_slot
    place_key = (place_key + span * place_block)[:, None]
    both_hot = (place_key == both_keys[0]) | (place_key == both_keys[1])
    pairs_out = jnp.dot(
        both_hot.astype(jnp.bfloat16), both_pairs, preferred_element_type=jnp.float32
    ).astype(jnp.bfloat16)
    pairs_out, _ = lax.optimization_barrier((pairs_out, kv_parts[1:-1]))
    pairs_in = lax.all_to_all(
        pairs_out.reshape(half, 2 * local_count * CAP, -1),
        "tm",
        split_axis=0,
        concat_axis=0,
        axis_index_groups=[list(range(half)), list(range(half, devices))],
        tiled=True,
    )
    pairs_in = pairs_in.reshape(half, 2, local_count, CAP, -1)

    placed = [
        jnp.dot(
            pairs_in[:, :, local].transpose(1, 0, 2, 3).reshape(slots, -1),
            conv_weight,
            preferred_element_type=jnp.float32,
        ).astype(jnp.bfloat16)
        for local in range(local_count)
    ]
    context_in = []
    for local in range(local_count):
        outgoing = spread(context, local)
        if local:
            outgoing, placed = lax.optimization_barrier((outgoing, placed))
        context_in.append(exchange(outgoing.reshape(devices, CAP, -1)).reshape(slots, -1))

    returned = []
    for local in range(local_count):
        mid = (
            placed[local].astype(jnp.float32)
            + jnp.dot(context_in[local], w_out, preferred_element_type=jnp.float32)
        ).astype(jnp.bfloat16)
        result = run_expert(mid, ffn_gain, expert_in, expert_out, local, local_count)
        returned.append(exchange(result.reshape(devices, CAP, feat_dim)).reshape(slots, feat_dim))

    stream_mid = (
        embedded.astype(jnp.float32) + jnp.dot(context, w_out, preferred_element_type=jnp.float32)
    ).astype(jnp.bfloat16)
    ffn_input = rms_scale(stream_mid.astype(jnp.float32), ffn_gain).astype(jnp.bfloat16)
    affinity = jax.nn.sigmoid(jnp.dot(ffn_input, router_w, preferred_element_type=jnp.float32))
    chosen_hot = expert_ids[:, :, None] == jnp.arange(experts, dtype=jnp.int32)[None, None, :]
    picked = jnp.sum(jnp.where(chosen_hot, affinity[:, None, :], 0.0), axis=-1)
    route_weight = picked / jnp.sum(picked, axis=1, keepdims=True)

    mixed = stream_mid.astype(jnp.float32)
    for local in range(local_count):
        kind = jnp.bfloat16 if local == local_count - 1 else jnp.float32
        mixed = combine(mixed, route_weight, route_key, row_keys[local], returned[local], kind)
    return mixed


def solution(mesh):
    placed = (
        P("tm", None),
        P(),
        P(),
        P(),
        P(),
        P(),
        P(),
        P(),
        P(),
        P(None, "tm", None),
        P("tm", None),
        P("tm", None),
        P("tm", None),
    )
    return jax.shard_map(
        shards, mesh=mesh, in_specs=placed, out_specs=P("tm", None), check_vma=False
    )
```

```python
import functools
import math

import jax
import jax.numpy as jnp
from jax import lax
from jax.experimental import pallas as pl
from jax.experimental.pallas import tpu as pltpu
from jax.sharding import PartitionSpec as P

HEAD_DIM = 128
WINDOW = 2048
CAP = 16

NORM_EPS = 1e-06
MASKED = -1e30


def from_behind(block, axis, distance):
    devices = range(lax.axis_size(axis))
    route = [(i - distance, i) for i in devices if i - distance in devices]
    return lax.ppermute(block, axis, route)


def rms_scale(values, gain_vec):
    mean_sq = jnp.mean(values * values, axis=-1, keepdims=True)
    return values * lax.rsqrt(mean_sq + NORM_EPS) * gain_vec


def head_norm(values):
    mean_sq = jnp.mean(values * values, axis=-1, keepdims=True)
    return values * lax.rsqrt(mean_sq + NORM_EPS)


def expert_body(steps, mid_ref, gain_ref, w_in_ref, w_out_ref, out_ref, rows_ref, total_ref):
    step = pl.program_id(1)

    @pl.when(step == 0)
    def _():
        mid = mid_ref[...].astype(jnp.float32)
        rows_ref[...] = rms_scale(mid, gain_ref[...]).astype(jnp.bfloat16)

    rows = rows_ref[...]
    nt = (((1,), (1,)), ((), ()))
    gate = lax.dot_general(rows, w_in_ref[0], nt, preferred_element_type=jnp.float32)
    up = lax.dot_general(rows, w_in_ref[1], nt, preferred_element_type=jnp.float32)
    hidden = (gate / (1.0 + jnp.exp(-gate)) * up).astype(jnp.bfloat16)
    part = jnp.dot(hidden, w_out_ref[...], preferred_element_type=jnp.float32)

    @pl.when(step == 0)
    def _():
        total_ref[...] = part

    @pl.when(step > 0)
    def _():
        total_ref[...] += part

    @pl.when(step == steps - 1)
    def _():
        out_ref[...] = total_ref[...].astype(out_ref.dtype)


def run_expert(mid, gain, expert_in, expert_out, local, local_count):
    row_total, feat_dim = mid.shape
    units = expert_out.shape[0] // local_count
    width = 352
    steps = units // width
    first = local * steps
    tile = math.gcd(row_total, 512)
    flops = 6 * row_total * units * feat_dim
    return pl.pallas_call(
        functools.partial(expert_body, steps),
        grid=(row_total // tile, steps),
        in_specs=[
            pl.BlockSpec((tile, feat_dim), lambda r, i: (r, 0)),
            pl.BlockSpec((1, feat_dim), lambda r, i: (0, 0)),
            pl.BlockSpec((2, width, feat_dim), lambda r, i: (0, first + i, 0)),
            pl.BlockSpec((width, feat_dim), lambda r, i: (first + i, 0)),
        ],
        out_specs=pl.BlockSpec((tile, feat_dim), lambda r, i: (r, 0)),
        out_shape=jax.ShapeDtypeStruct((row_total, feat_dim), jnp.bfloat16),
        scratch_shapes=[
            pltpu.VMEM((tile, feat_dim), jnp.bfloat16),
            pltpu.VMEM((tile, feat_dim), jnp.float32),
        ],
        compiler_params=pltpu.CompilerParams(vmem_limit_bytes=40 << 20),
        cost_estimate=pl.CostEstimate(
            flops=flops,
            bytes_accessed=6 * units * feat_dim + 4 * row_total * feat_dim,
            transcendentals=row_total * units,
        ),
    )(mid, gain.reshape(1, -1), expert_in, expert_out)


def spread_body(
    shape, info_ref, signal_ref, before_ref, key_ref, far_ref, out_ref
):
    half, copies, local_count, count = shape
    rows = out_ref.shape[0]
    tokens, width = signal_ref.shape
    first_dev, own_block = info_ref[0], info_ref[1]
    row = pl.program_id(0) * rows + lax.broadcasted_iota(jnp.int32, (rows, 1), 0)
    slot = lax.rem(row, CAP)
    local = lax.rem(lax.div(row, CAP), local_count)
    block = lax.rem(lax.div(row, CAP * local_count), 2)
    dev = first_dev + lax.div(row, CAP * local_count * 2)
    want = ((lax.div(dev, copies) * local_count + local) * CAP + slot).astype(jnp.float32)
    lane = lax.broadcasted_iota(jnp.int32, (8, tokens), 1)

    own_keys = [key_ref[route : route + 1].astype(jnp.float32) for route in range(2)]
    far_rows = [far_ref[tokens + 1 + at : tokens + 2 + at].astype(jnp.float32) for at in range(2)]
    far_all = far_rows[0] * CAP + far_rows[1]
    far_keys = [far_all[:, route * tokens : (route + 1) * tokens] for route in range(2)]
    far_before = far_ref[tokens : tokens + 1]
    now = jnp.zeros((rows, width), jnp.float32)
    past = jnp.zeros((rows, width), jnp.float32)
    for mine, keys, samples, before in (
        (True, own_keys, signal_ref[...], before_ref[...]),
        (False, far_keys, far_ref[:tokens], far_before),
    ):
        here = (block == own_block) if mine else (block != own_block)
        sought = jnp.where(here, want, -1.0)
        hot, hot_next, hot_first = False, False, False
        for key in keys:
            wide = jnp.broadcast_to(key, (8, tokens))
            after = jnp.where(lane == tokens - 1, -2.0, pltpu.roll(wide, tokens - 1, 1))[:1]
            hot = (sought == key) | hot
            hot_next = (sought == after) | hot_next
            hot_first = (sought == key[:, :1]) | hot_first
        now += jnp.dot(hot.astype(jnp.bfloat16), samples, preferred_element_type=jnp.float32)
        past += jnp.dot(
            hot_next.astype(jnp.bfloat16), samples, preferred_element_type=jnp.float32
        )
        past += jnp.where(hot_first, before.astype(jnp.float32), 0.0)
    out_ref[:, :width] = past.astype(out_ref.dtype)
    out_ref[:, width:] = now.astype(out_ref.dtype)


def spread_pairs(info, signal, before, keys, far, half, copies, local_count):
    tokens, width = signal.shape
    rows = half * 2 * local_count * CAP
    tile = math.gcd(rows, 256)
    whole = lambda shape: pl.BlockSpec(shape, lambda i: (0, 0))
    return pl.pallas_call(
        functools.partial(spread_body, (half, copies, local_count, tokens)),
        grid=(rows // tile,),
        in_specs=[
            pl.BlockSpec(memory_space=pltpu.SMEM),
            whole(signal.shape),
            whole(before.shape),
            whole(keys.shape),
            whole(far.shape),
        ],
        out_specs=pl.BlockSpec((tile, 2 * width), lambda i: (i, 0)),
        out_shape=jax.ShapeDtypeStruct((rows, 2 * width), jnp.bfloat16),
        compiler_params=pltpu.CompilerParams(vmem_limit_bytes=16 << 20),
        cost_estimate=pl.CostEstimate(
            flops=8 * rows * tokens * width,
            bytes_accessed=4 * rows * width + 4 * tokens * width,
            transcendentals=0,
        ),
    )(info, signal, before, keys, far)


def combine_body(base_ref, weight_ref, key_ref, row_ref, rows_ref, out_ref):
    total = base_ref[...]
    for route in range(2):
        hot = (key_ref[:, route : route + 1] == row_ref[...]).astype(jnp.bfloat16)
        rows = jnp.dot(hot, rows_ref[...], preferred_element_type=jnp.float32)
        rows = rows.astype(jnp.bfloat16).astype(jnp.float32)
        total = total + weight_ref[:, route : route + 1] * rows
    out_ref[...] = total.astype(out_ref.dtype)


def combine(base, weight, key, row_key, rows, kind):
    row_count, feat_dim = base.shape
    slots = rows.shape[0]
    width = math.gcd(feat_dim, 512)
    return pl.pallas_call(
        combine_body,
        grid=(feat_dim // width,),
        in_specs=[
            pl.BlockSpec((row_count, width), lambda i: (0, i)),
            pl.BlockSpec((row_count, 2), lambda i: (0, 0)),
            pl.BlockSpec((row_count, 2), lambda i: (0, 0)),
            pl.BlockSpec((1, slots), lambda i: (0, 0)),
            pl.BlockSpec((slots, width), lambda i: (0, i)),
        ],
        out_specs=pl.BlockSpec((row_count, width), lambda i: (0, i)),
        out_shape=jax.ShapeDtypeStruct((row_count, feat_dim), kind),
        compiler_params=pltpu.CompilerParams(vmem_limit_bytes=24 << 20),
        cost_estimate=pl.CostEstimate(
            flops=4 * row_count * slots * feat_dim,
            bytes_accessed=2 * slots * feat_dim + 8 * row_count * feat_dim,
            transcendentals=0,
        ),
    )(base, weight, key, row_key.reshape(1, -1), rows)


def kv_body(rows_ref, weight_ref, out_ref):
    both = jnp.dot(rows_ref[...], weight_ref[...], preferred_element_type=jnp.float32)
    kv_dim = both.shape[1] // 2
    for start in range(0, kv_dim, HEAD_DIM):
        head = both[:, start : start + HEAD_DIM]
        out_ref[:, start : start + HEAD_DIM] = head_norm(head).astype(out_ref.dtype)
    out_ref[:, kv_dim:] = both[:, kv_dim:].astype(out_ref.dtype)


def project_kv(rows, weight):
    row_count, feat_dim = rows.shape
    width = weight.shape[1]
    return pl.pallas_call(
        kv_body,
        out_shape=jax.ShapeDtypeStruct((row_count, width), jnp.bfloat16),
        in_specs=[pl.BlockSpec(memory_space=pltpu.VMEM)] * 2,
        out_specs=pl.BlockSpec(memory_space=pltpu.VMEM),
        compiler_params=pltpu.CompilerParams(vmem_limit_bytes=16 << 20),
        cost_estimate=pl.CostEstimate(
            flops=2 * row_count * feat_dim * width,
            bytes_accessed=2 * (row_count * feat_dim + feat_dim * width),
            transcendentals=row_count,
        ),
    )(rows, weight)


def attend_body(kv_heads, flag_ref, scale_ref, query_ref, *refs):
    *kv_refs, out_ref, unit_ref, key_ref, value_ref, score_ref = refs
    blocks = [ref.at[part] for ref in kv_refs for part in range(ref.shape[0])]
    rows = query_ref.shape[0]
    heads = query_ref.shape[1] // HEAD_DIM
    group = heads // kv_heads
    kv_dim = kv_heads * HEAD_DIM
    count = len(blocks)
    for pos, block in enumerate(blocks):
        for kv in range(kv_heads):
            low = kv * HEAD_DIM
            key_ref[kv, pos] = block[:, low : low + HEAD_DIM]
            value_ref[kv, pos, :, :HEAD_DIM] = block[:, kv_dim + low : kv_dim + low + HEAD_DIM]
    for kv in range(kv_heads):
        for pos in range(count):
            value_ref[kv, pos, :, HEAD_DIM:] = jnp.ones((rows, HEAD_DIM), jnp.bfloat16)
    for head in range(heads):
        unit_ref[head] = head_norm(
            query_ref[:, head * HEAD_DIM : (head + 1) * HEAD_DIM]
        ).astype(jnp.bfloat16)
    query_at = lax.broadcasted_iota(jnp.int32, (rows, rows), 0)
    key_at = lax.broadcasted_iota(jnp.int32, (rows, rows), 1)

    @pl.loop(0, heads)
    def _(head):
        kv = head // group
        unit = unit_ref[head]
        top = jnp.full((rows, HEAD_DIM), MASKED, jnp.float32)
        for pos in range(count):
            score = lax.dot_general(
                unit,
                key_ref[kv, pos],
                (((1,), (1,)), ((), ())),
                preferred_element_type=jnp.float32,
            )
            if pos == 0:
                score = jnp.where(key_at <= query_at, score, MASKED)
            if pos == 1:
                score = jnp.where(key_at > query_at, score, MASKED)
            score_ref[pos] = score
            high = score[:, :HEAD_DIM]
            for low in range(HEAD_DIM, rows, HEAD_DIM):
                high = jnp.maximum(high, score[:, low : low + HEAD_DIM])
            if pos:
                high = jnp.where(flag_ref[pos] > 0, high, MASKED)
            top = jnp.maximum(top, high)
        factor = scale_ref[head] * (math.log2(math.e) / math.sqrt(HEAD_DIM))
        top = jnp.max(top, axis=1, keepdims=True)
        total = jnp.zeros((rows, 2 * HEAD_DIM), jnp.float32)
        for pos in range(count):
            base = jnp.where(flag_ref[pos] > 0, top, -MASKED) if pos else top
            weight = jnp.exp2((score_ref[pos] - base) * factor).astype(jnp.bfloat16)
            total += jnp.dot(weight, value_ref[kv, pos], preferred_element_type=jnp.float32)
        place_at = pl.ds(pl.multiple_of(head * HEAD_DIM, HEAD_DIM), HEAD_DIM)
        out_ref[:, place_at] = (total[:, :HEAD_DIM] / total[:, HEAD_DIM:]).astype(out_ref.dtype)


def attend(flags, head_scale, queries, kv_parts, kv_heads):
    rows, width = queries.shape
    heads = width // HEAD_DIM
    count = flags.shape[0]
    smem = pl.BlockSpec(memory_space=pltpu.SMEM)
    vmem = pl.BlockSpec(memory_space=pltpu.VMEM)
    return pl.pallas_call(
        functools.partial(attend_body, kv_heads),
        out_shape=jax.ShapeDtypeStruct((rows, width), jnp.bfloat16),
        in_specs=[smem, smem, vmem] + [vmem] * len(kv_parts),
        out_specs=vmem,
        scratch_shapes=[
            pltpu.VMEM((heads, rows, HEAD_DIM), jnp.bfloat16),
            pltpu.VMEM((kv_heads, count, rows, HEAD_DIM), jnp.bfloat16),
            pltpu.VMEM((kv_heads, count, rows, 2 * HEAD_DIM), jnp.bfloat16),
            pltpu.VMEM((count, rows, rows), jnp.float32),
        ],
        compiler_params=pltpu.CompilerParams(vmem_limit_bytes=32 << 20),
        cost_estimate=pl.CostEstimate(
            flops=6 * heads * count * rows * rows * HEAD_DIM,
            bytes_accessed=rows * width * 6 + count * rows * kv_heads * HEAD_DIM * 4,
            transcendentals=heads * count * rows * rows,
        ),
    )(flags, head_scale, queries, *kv_parts)


def window_parts(own_kv, prior_kv, group):
    devices = lax.axis_size("tm")
    me = lax.axis_index("tm")
    core, chip, base = me % 2, me % group // 2, me // group * group
    fetched, flags, sent = [], [], []
    for step in range(1, group // 2):
        other = chip ^ step
        block = jnp.where(other > chip, own_kv, prior_kv)
        sent.append(block)
        fetched.append(
            lax.ppermute(block, "tm", [(dev, dev ^ (2 * step)) for dev in range(devices)])
        )
        flags.append((other < chip) | (base > 0))
    shared = jnp.stack(fetched + [jnp.where(core == 0, own_kv, prior_kv)])
    shared = lax.ppermute(shared, "tm", [(dev, dev ^ 1) for dev in range(devices)])
    flags = [me >= 0, base > 0] + flags + flags + [(core > 0) | (base > 0)]
    parts = [block[None] for block in [own_kv, prior_kv] + fetched] + [shared]
    return parts, jnp.stack(flags).astype(jnp.int32), sent


def shards(
    signal,
    conv_weight,
    attn_gain,
    w_query,
    w_keyval,
    w_out,
    head_scale,
    ffn_gain,
    router_w,
    expert_in,
    expert_out,
    expert_ids,
    slot_ids,
):
    row_count = signal.shape[0]
    feat_dim = conv_weight.shape[1]
    devices = lax.axis_size("tm")
    dev_index = lax.axis_index("tm")
    experts = router_w.shape[1]
    copies = max(devices // experts, 1)
    local_count = max(experts // devices, 1)
    slots = devices * CAP

    route_key = expert_ids * CAP + slot_ids
    row_id = jnp.arange(slots, dtype=jnp.int32)
    row_dev, row_slot = row_id // CAP, row_id % CAP
    row_keys = [
        (row_dev // copies * local_count + local) * CAP + row_slot for local in range(local_count)
    ]

    def spread(values, local):
        hot = (row_keys[local][:, None] == route_key[None, :, 0]) | (
            row_keys[local][:, None] == route_key[None, :, 1]
        )
        return jnp.dot(
            hot.astype(jnp.bfloat16), values, preferred_element_type=jnp.float32
        ).astype(jnp.bfloat16)

    def exchange(rows):
        return lax.all_to_all(rows, "tm", split_axis=0, concat_axis=0, tiled=True)

    reach_blocks = WINDOW // row_count
    group = reach_blocks
    before = from_behind(signal[row_count - 1 :], "tm", 1)
    half = devices // 2
    routes = [
        table.astype(jnp.bfloat16).T.reshape(-1, signal.shape[1]) for table in (expert_ids, slot_ids)
    ]
    ahead = jnp.concatenate([signal, before] + routes, axis=0)
    used = ahead.shape[0]
    ahead = jnp.pad(ahead, ((0, -used % 16), (0, 0)))
    prior = from_behind(ahead, "tm", group)
    ahead, prior = lax.optimization_barrier((ahead, prior))
    far = lax.ppermute(ahead, "tm", [(dev, (dev + half) % devices) for dev in range(devices)])

    def pairs_of(block, first):
        return jnp.concatenate([jnp.concatenate([first, block[:-1]], axis=0), block], axis=1)

    def embed(pairs):
        rows = jnp.dot(pairs, conv_weight, preferred_element_type=jnp.float32)
        return rows.astype(jnp.bfloat16)

    def norm_rows(rows):
        return rms_scale(rows.astype(jnp.float32), attn_gain).astype(jnp.bfloat16)

    patch_pairs = pairs_of(signal, before)
    embedded = embed(patch_pairs)
    normed = norm_rows(embedded)
    kv_heads = w_keyval.shape[1] // 2 // HEAD_DIM
    own_kv = project_kv(normed, w_keyval)
    prior_pairs = pairs_of(prior[:row_count], prior[row_count : row_count + 1])
    prior_kv = project_kv(norm_rows(embed(prior_pairs)), w_keyval)
    kv_parts, flags, sent = window_parts(own_kv, prior_kv, group)
    queries = jnp.dot(normed, w_query, preferred_element_type=jnp.float32)
    context = attend(flags, head_scale, queries, kv_parts, kv_heads)

    far, _ = lax.optimization_barrier((far, sent))
    in_first = dev_index < half
    info = jnp.stack([jnp.where(in_first, 0, half), jnp.where(in_first, 0, 1)]).astype(jnp.int32)
    pairs_out = spread_pairs(info, signal, before, route_key.T, far, half, copies, local_count)
    pairs_out, _ = lax.optimization_barrier((pairs_out, kv_parts[2:-1]))
    pairs_in = lax.all_to_all(
        pairs_out.reshape(half, 2 * local_count * CAP, -1),
        "tm",
        split_axis=0,
        concat_axis=0,
        axis_index_groups=[list(range(half)), list(range(half, devices))],
        tiled=True,
    )
    pairs_in = pairs_in.reshape(half, 2, local_count, CAP, -1)

    placed = [
        embed(pairs_in[:, :, local].transpose(1, 0, 2, 3).reshape(slots, -1))
        for local in range(local_count)
    ]
    context_in = []
    for local in range(local_count):
        outgoing = spread(context, local)
        if local:
            outgoing, placed = lax.optimization_barrier((outgoing, placed))
        context_in.append(exchange(outgoing.reshape(devices, CAP, -1)).reshape(slots, -1))

    returned = []
    for local in range(local_count):
        mid = (
            placed[local].astype(jnp.float32)
            + jnp.dot(context_in[local], w_out, preferred_element_type=jnp.float32)
        ).astype(jnp.bfloat16)
        result = run_expert(mid, ffn_gain, expert_in, expert_out, local, local_count)
        returned.append(exchange(result.reshape(devices, CAP, feat_dim)).reshape(slots, feat_dim))

    expert_ids, slot_ids, _ = lax.optimization_barrier((expert_ids, slot_ids, context))
    route_key = expert_ids * CAP + slot_ids
    stream_mid = (
        embedded.astype(jnp.float32) + jnp.dot(context, w_out, preferred_element_type=jnp.float32)
    ).astype(jnp.bfloat16)
    ffn_input = rms_scale(stream_mid.astype(jnp.float32), ffn_gain).astype(jnp.bfloat16)
    affinity = jax.nn.sigmoid(jnp.dot(ffn_input, router_w, preferred_element_type=jnp.float32))
    chosen_hot = expert_ids[:, :, None] == jnp.arange(experts, dtype=jnp.int32)[None, None, :]
    picked = jnp.sum(jnp.where(chosen_hot, affinity[:, None, :], 0.0), axis=-1)
    route_weight = picked / jnp.sum(picked, axis=1, keepdims=True)

    mixed = stream_mid.astype(jnp.float32)
    for local in range(local_count):
        kind = jnp.bfloat16 if local == local_count - 1 else jnp.float32
        mixed = combine(mixed, route_weight, route_key, row_keys[local], returned[local], kind)
    return mixed


def solution(mesh):
    placed = (
        P("tm", None),
        P(),
        P(),
        P(),
        P(),
        P(),
        P(),
        P(),
        P(),
        P(None, "tm", None),
        P("tm", None),
        P("tm", None),
        P("tm", None),
    )
    return jax.shard_map(
        shards, mesh=mesh, in_specs=placed, out_specs=P("tm", None), check_vma=False
    )
```

```python
import functools
import math

import jax
import jax.numpy as jnp
from jax import lax
from jax.experimental import pallas as pl
from jax.experimental.pallas import tpu as pltpu
from jax.sharding import PartitionSpec as P

HEAD_DIM = 128
WINDOW = 2048
CAP = 16

NORM_EPS = 1e-06
MASKED = -1e30


def from_behind(block, axis, distance):
    devices = range(lax.axis_size(axis))
    route = [(i - distance, i) for i in devices if i - distance in devices]
    return lax.ppermute(block, axis, route)


def rms_scale(values, gain_vec):
    mean_sq = jnp.mean(values * values, axis=-1, keepdims=True)
    return values * lax.rsqrt(mean_sq + NORM_EPS) * gain_vec


def head_norm(values):
    mean_sq = jnp.mean(values * values, axis=-1, keepdims=True)
    return values * lax.rsqrt(mean_sq + NORM_EPS)


def expert_body(steps, mid_ref, gain_ref, w_in_ref, w_out_ref, out_ref, rows_ref, total_ref):
    step = pl.program_id(1)

    @pl.when(step == 0)
    def _():
        mid = mid_ref[...].astype(jnp.float32)
        rows_ref[...] = rms_scale(mid, gain_ref[...]).astype(jnp.bfloat16)

    rows = rows_ref[...]
    nt = (((1,), (1,)), ((), ()))
    gate = lax.dot_general(rows, w_in_ref[0], nt, preferred_element_type=jnp.float32)
    up = lax.dot_general(rows, w_in_ref[1], nt, preferred_element_type=jnp.float32)
    hidden = (gate / (1.0 + jnp.exp(-gate)) * up).astype(jnp.bfloat16)
    part = jnp.dot(hidden, w_out_ref[...], preferred_element_type=jnp.float32)

    @pl.when(step == 0)
    def _():
        total_ref[...] = part

    @pl.when(step > 0)
    def _():
        total_ref[...] += part

    @pl.when(step == steps - 1)
    def _():
        out_ref[...] = total_ref[...].astype(out_ref.dtype)


def run_expert(mid, gain, expert_in, expert_out, local, local_count):
    row_total, feat_dim = mid.shape
    units = expert_out.shape[0] // local_count
    width = 352
    steps = units // width
    first = local * steps
    tile = math.gcd(row_total, 512)
    flops = 6 * row_total * units * feat_dim
    return pl.pallas_call(
        functools.partial(expert_body, steps),
        grid=(row_total // tile, steps),
        in_specs=[
            pl.BlockSpec((tile, feat_dim), lambda r, i: (r, 0)),
            pl.BlockSpec((1, feat_dim), lambda r, i: (0, 0)),
            pl.BlockSpec((2, width, feat_dim), lambda r, i: (0, first + i, 0)),
            pl.BlockSpec((width, feat_dim), lambda r, i: (first + i, 0)),
        ],
        out_specs=pl.BlockSpec((tile, feat_dim), lambda r, i: (r, 0)),
        out_shape=jax.ShapeDtypeStruct((row_total, feat_dim), jnp.bfloat16),
        scratch_shapes=[
            pltpu.VMEM((tile, feat_dim), jnp.bfloat16),
            pltpu.VMEM((tile, feat_dim), jnp.float32),
        ],
        compiler_params=pltpu.CompilerParams(vmem_limit_bytes=40 << 20),
        cost_estimate=pl.CostEstimate(
            flops=flops,
            bytes_accessed=6 * units * feat_dim + 4 * row_total * feat_dim,
            transcendentals=row_total * units,
        ),
    )(mid, gain.reshape(1, -1), expert_in, expert_out)


def spread_body(
    shape, info_ref, signal_ref, before_ref, key_ref, far_ref, out_ref
):
    half, copies, local_count, count = shape
    rows = out_ref.shape[0]
    tokens, width = signal_ref.shape
    first_dev, own_block = info_ref[0], info_ref[1]
    row = pl.program_id(0) * rows + lax.broadcasted_iota(jnp.int32, (rows, 1), 0)
    slot = lax.rem(row, CAP)
    local = lax.rem(lax.div(row, CAP), local_count)
    block = lax.rem(lax.div(row, CAP * local_count), 2)
    dev = first_dev + lax.div(row, CAP * local_count * 2)
    want = ((lax.div(dev, copies) * local_count + local) * CAP + slot).astype(jnp.float32)
    lane = lax.broadcasted_iota(jnp.int32, (8, tokens), 1)

    own_keys = [key_ref[route : route + 1].astype(jnp.float32) for route in range(2)]
    far_rows = [far_ref[tokens + 1 + at : tokens + 2 + at].astype(jnp.float32) for at in range(2)]
    far_all = far_rows[0] * CAP + far_rows[1]
    far_keys = [far_all[:, route * tokens : (route + 1) * tokens] for route in range(2)]
    far_before = far_ref[tokens : tokens + 1]
    now = jnp.zeros((rows, width), jnp.float32)
    past = jnp.zeros((rows, width), jnp.float32)
    for mine, keys, samples, before in (
        (True, own_keys, signal_ref[...], before_ref[...]),
        (False, far_keys, far_ref[:tokens], far_before),
    ):
        here = (block == own_block) if mine else (block != own_block)
        sought = jnp.where(here, want, -1.0)
        hot, hot_next, hot_first = False, False, False
        for key in keys:
            wide = jnp.broadcast_to(key, (8, tokens))
            after = jnp.where(lane == tokens - 1, -2.0, pltpu.roll(wide, tokens - 1, 1))[:1]
            hot = (sought == key) | hot
            hot_next = (sought == after) | hot_next
            hot_first = (sought == key[:, :1]) | hot_first
        now += jnp.dot(hot.astype(jnp.bfloat16), samples, preferred_element_type=jnp.float32)
        past += jnp.dot(
            hot_next.astype(jnp.bfloat16), samples, preferred_element_type=jnp.float32
        )
        past += jnp.where(hot_first, before.astype(jnp.float32), 0.0)
    out_ref[:, :width] = past.astype(out_ref.dtype)
    out_ref[:, width:] = now.astype(out_ref.dtype)


def spread_pairs(info, signal, before, keys, far, half, copies, local_count):
    tokens, width = signal.shape
    rows = half * 2 * local_count * CAP
    tile = math.gcd(rows, 256)
    whole = lambda shape: pl.BlockSpec(shape, lambda i: (0, 0))
    return pl.pallas_call(
        functools.partial(spread_body, (half, copies, local_count, tokens)),
        grid=(rows // tile,),
        in_specs=[
            pl.BlockSpec(memory_space=pltpu.SMEM),
            whole(signal.shape),
            whole(before.shape),
            whole(keys.shape),
            whole(far.shape),
        ],
        out_specs=pl.BlockSpec((tile, 2 * width), lambda i: (i, 0)),
        out_shape=jax.ShapeDtypeStruct((rows, 2 * width), jnp.bfloat16),
        compiler_params=pltpu.CompilerParams(vmem_limit_bytes=16 << 20),
        cost_estimate=pl.CostEstimate(
            flops=8 * rows * tokens * width,
            bytes_accessed=4 * rows * width + 4 * tokens * width,
            transcendentals=0,
        ),
    )(info, signal, before, keys, far)


def combine_body(base_ref, weight_ref, key_ref, row_ref, rows_ref, out_ref, hot_ref):
    @pl.when(pl.program_id(0) == 0)
    def _():
        for route in range(2):
            hot = key_ref[:, route : route + 1] == row_ref[...]
            hot_ref[route] = hot.astype(jnp.bfloat16)

    total = base_ref[...]
    for route in range(2):
        rows = jnp.dot(hot_ref[route], rows_ref[...], preferred_element_type=jnp.float32)
        rows = rows.astype(jnp.bfloat16).astype(jnp.float32)
        total = total + weight_ref[:, route : route + 1] * rows
    out_ref[...] = total.astype(out_ref.dtype)


def combine(base, weight, key, row_key, rows, kind):
    row_count, feat_dim = base.shape
    slots = rows.shape[0]
    width = math.gcd(feat_dim, 512)
    return pl.pallas_call(
        combine_body,
        grid=(feat_dim // width,),
        in_specs=[
            pl.BlockSpec((row_count, width), lambda i: (0, i)),
            pl.BlockSpec((row_count, 2), lambda i: (0, 0)),
            pl.BlockSpec((row_count, 2), lambda i: (0, 0)),
            pl.BlockSpec((1, slots), lambda i: (0, 0)),
            pl.BlockSpec((slots, width), lambda i: (0, i)),
        ],
        out_specs=pl.BlockSpec((row_count, width), lambda i: (0, i)),
        out_shape=jax.ShapeDtypeStruct((row_count, feat_dim), kind),
        scratch_shapes=[pltpu.VMEM((2, row_count, slots), jnp.bfloat16)],
        compiler_params=pltpu.CompilerParams(vmem_limit_bytes=24 << 20),
        cost_estimate=pl.CostEstimate(
            flops=4 * row_count * slots * feat_dim,
            bytes_accessed=2 * slots * feat_dim + 8 * row_count * feat_dim,
            transcendentals=0,
        ),
    )(base, weight, key, row_key.reshape(1, -1), pltpu.with_memory_space_constraint(rows, pltpu.HBM))


def kv_body(rows_ref, weight_ref, out_ref):
    both = jnp.dot(rows_ref[...], weight_ref[...], preferred_element_type=jnp.float32)
    kv_dim = both.shape[1] // 2
    for start in range(0, kv_dim, HEAD_DIM):
        head = both[:, start : start + HEAD_DIM]
        out_ref[:, start : start + HEAD_DIM] = head_norm(head).astype(out_ref.dtype)
    out_ref[:, kv_dim:] = both[:, kv_dim:].astype(out_ref.dtype)


def project_kv(rows, weight):
    row_count, feat_dim = rows.shape
    width = weight.shape[1]
    return pl.pallas_call(
        kv_body,
        out_shape=jax.ShapeDtypeStruct((row_count, width), jnp.bfloat16),
        in_specs=[pl.BlockSpec(memory_space=pltpu.VMEM)] * 2,
        out_specs=pl.BlockSpec(memory_space=pltpu.VMEM),
        compiler_params=pltpu.CompilerParams(vmem_limit_bytes=16 << 20),
        cost_estimate=pl.CostEstimate(
            flops=2 * row_count * feat_dim * width,
            bytes_accessed=2 * (row_count * feat_dim + feat_dim * width),
            transcendentals=row_count,
        ),
    )(rows, weight)


def attend_body(kv_heads, flag_ref, scale_ref, query_ref, *refs):
    *kv_refs, out_ref, unit_ref, key_ref, value_ref, score_ref = refs
    blocks = [ref.at[part] for ref in kv_refs for part in range(ref.shape[0])]
    rows = query_ref.shape[0]
    heads = query_ref.shape[1] // HEAD_DIM
    group = heads // kv_heads
    kv_dim = kv_heads * HEAD_DIM
    count = len(blocks)
    for pos, block in enumerate(blocks):
        for kv in range(kv_heads):
            low = kv * HEAD_DIM
            key_ref[kv, pos] = block[:, low : low + HEAD_DIM]
            value_ref[kv, pos, :, :HEAD_DIM] = block[:, kv_dim + low : kv_dim + low + HEAD_DIM]
    for kv in range(kv_heads):
        for pos in range(count):
            value_ref[kv, pos, :, HEAD_DIM:] = jnp.ones((rows, HEAD_DIM), jnp.bfloat16)
    for head in range(heads):
        unit_ref[head] = head_norm(
            query_ref[:, head * HEAD_DIM : (head + 1) * HEAD_DIM]
        ).astype(jnp.bfloat16)
    query_at = lax.broadcasted_iota(jnp.int32, (rows, rows), 0)
    key_at = lax.broadcasted_iota(jnp.int32, (rows, rows), 1)

    @pl.loop(0, heads)
    def _(head):
        kv = head // group
        unit = unit_ref[head]
        top = jnp.full((rows, HEAD_DIM), MASKED, jnp.float32)
        for pos in range(count):
            score = lax.dot_general(
                unit,
                key_ref[kv, pos],
                (((1,), (1,)), ((), ())),
                preferred_element_type=jnp.float32,
            )
            if pos == 0:
                score = jnp.where(key_at <= query_at, score, MASKED)
            if pos == 1:
                score = jnp.where(key_at > query_at, score, MASKED)
            score_ref[pos] = score
            high = score[:, :HEAD_DIM]
            for low in range(HEAD_DIM, rows, HEAD_DIM):
                high = jnp.maximum(high, score[:, low : low + HEAD_DIM])
            if pos:
                high = jnp.where(flag_ref[pos] > 0, high, MASKED)
            top = jnp.maximum(top, high)
        factor = scale_ref[head] * (math.log2(math.e) / math.sqrt(HEAD_DIM))
        top = jnp.max(top, axis=1, keepdims=True)
        total = jnp.zeros((rows, 2 * HEAD_DIM), jnp.float32)
        for pos in range(count):
            base = jnp.where(flag_ref[pos] > 0, top, -MASKED) if pos else top
            weight = jnp.exp2((score_ref[pos] - base) * factor).astype(jnp.bfloat16)
            total += jnp.dot(weight, value_ref[kv, pos], preferred_element_type=jnp.float32)
        place_at = pl.ds(pl.multiple_of(head * HEAD_DIM, HEAD_DIM), HEAD_DIM)
        out_ref[:, place_at] = (total[:, :HEAD_DIM] / total[:, HEAD_DIM:]).astype(out_ref.dtype)


def attend(flags, head_scale, queries, kv_parts, kv_heads):
    rows, width = queries.shape
    heads = width // HEAD_DIM
    count = flags.shape[0]
    smem = pl.BlockSpec(memory_space=pltpu.SMEM)
    vmem = pl.BlockSpec(memory_space=pltpu.VMEM)
    return pl.pallas_call(
        functools.partial(attend_body, kv_heads),
        out_shape=jax.ShapeDtypeStruct((rows, width), jnp.bfloat16),
        in_specs=[smem, smem, vmem] + [vmem] * len(kv_parts),
        out_specs=vmem,
        scratch_shapes=[
            pltpu.VMEM((heads, rows, HEAD_DIM), jnp.bfloat16),
            pltpu.VMEM((kv_heads, count, rows, HEAD_DIM), jnp.bfloat16),
            pltpu.VMEM((kv_heads, count, rows, 2 * HEAD_DIM), jnp.bfloat16),
            pltpu.VMEM((count, rows, rows), jnp.float32),
        ],
        compiler_params=pltpu.CompilerParams(vmem_limit_bytes=32 << 20),
        cost_estimate=pl.CostEstimate(
            flops=6 * heads * count * rows * rows * HEAD_DIM,
            bytes_accessed=rows * width * 6 + count * rows * kv_heads * HEAD_DIM * 4,
            transcendentals=heads * count * rows * rows,
        ),
    )(flags, head_scale, queries, *kv_parts)


def window_parts(own_kv, prior_kv, group):
    devices = lax.axis_size("tm")
    me = lax.axis_index("tm")
    core, chip, base = me % 2, me % group // 2, me // group * group
    fetched, flags, sent = [], [], []
    for step in range(1, group // 2):
        other = chip ^ step
        block = jnp.where(other > chip, own_kv, prior_kv)
        sent.append(block)
        fetched.append(
            lax.ppermute(block, "tm", [(dev, dev ^ (2 * step)) for dev in range(devices)])
        )
        flags.append((other < chip) | (base > 0))
    shared = jnp.stack(fetched + [jnp.where(core == 0, own_kv, prior_kv)])
    shared = lax.ppermute(shared, "tm", [(dev, dev ^ 1) for dev in range(devices)])
    flags = [me >= 0, base > 0] + flags + flags + [(core > 0) | (base > 0)]
    parts = [block[None] for block in [own_kv, prior_kv] + fetched] + [shared]
    return parts, jnp.stack(flags).astype(jnp.int32), sent


def shards(
    signal,
    conv_weight,
    attn_gain,
    w_query,
    w_keyval,
    w_out,
    head_scale,
    ffn_gain,
    router_w,
    expert_in,
    expert_out,
    expert_ids,
    slot_ids,
):
    row_count = signal.shape[0]
    feat_dim = conv_weight.shape[1]
    devices = lax.axis_size("tm")
    dev_index = lax.axis_index("tm")
    experts = router_w.shape[1]
    copies = max(devices // experts, 1)
    local_count = max(experts // devices, 1)
    slots = devices * CAP

    route_key = expert_ids * CAP + slot_ids
    row_id = jnp.arange(slots, dtype=jnp.int32)
    row_dev, row_slot = row_id // CAP, row_id % CAP
    row_keys = [
        (row_dev // copies * local_count + local) * CAP + row_slot for local in range(local_count)
    ]

    def spread(values, local):
        hot = (row_keys[local][:, None] == route_key[None, :, 0]) | (
            row_keys[local][:, None] == route_key[None, :, 1]
        )
        return jnp.dot(
            hot.astype(jnp.bfloat16), values, preferred_element_type=jnp.float32
        ).astype(jnp.bfloat16)

    def exchange(rows):
        return lax.all_to_all(rows, "tm", split_axis=0, concat_axis=0, tiled=True)

    reach_blocks = WINDOW // row_count
    group = reach_blocks
    before = from_behind(signal[row_count - 1 :], "tm", 1)
    prior = from_behind(signal, "tm", group)
    prior_before = from_behind(signal[row_count - 1 :], "tm", group + 1)
    half = devices // 2
    routes = [
        table.astype(jnp.bfloat16).T.reshape(-1, signal.shape[1]) for table in (expert_ids, slot_ids)
    ]
    ahead = jnp.concatenate([signal, before] + routes, axis=0)
    ahead = jnp.pad(ahead, ((0, -ahead.shape[0] % 16), (0, 0)))
    far = lax.ppermute(ahead, "tm", [(dev, (dev + half) % devices) for dev in range(devices)])

    def pairs_of(block, first):
        return jnp.concatenate([jnp.concatenate([first, block[:-1]], axis=0), block], axis=1)

    def embed(pairs):
        rows = jnp.dot(pairs, conv_weight, preferred_element_type=jnp.float32)
        return rows.astype(jnp.bfloat16)

    def norm_rows(rows):
        return rms_scale(rows.astype(jnp.float32), attn_gain).astype(jnp.bfloat16)

    patch_pairs = pairs_of(signal, before)
    embedded = embed(patch_pairs)
    normed = norm_rows(embedded)
    kv_heads = w_keyval.shape[1] // 2 // HEAD_DIM
    own_kv = project_kv(normed, w_keyval)
    prior_pairs = pairs_of(prior, prior_before)
    prior_kv = project_kv(norm_rows(embed(prior_pairs)), w_keyval)
    kv_parts, flags, sent = window_parts(own_kv, prior_kv, group)
    queries = jnp.dot(normed, w_query, preferred_element_type=jnp.float32)
    context = attend(flags, head_scale, queries, kv_parts, kv_heads)

    far, _ = lax.optimization_barrier((far, sent))
    in_first = dev_index < half
    info = jnp.stack([jnp.where(in_first, 0, half), jnp.where(in_first, 0, 1)]).astype(jnp.int32)
    pairs_out = spread_pairs(info, signal, before, route_key.T, far, half, copies, local_count)
    pairs_out, _ = lax.optimization_barrier((pairs_out, kv_parts[2:-1]))
    pairs_in = lax.all_to_all(
        pairs_out.reshape(half, 2 * local_count * CAP, -1),
        "tm",
        split_axis=0,
        concat_axis=0,
        axis_index_groups=[list(range(half)), list(range(half, devices))],
        tiled=True,
    )
    pairs_in = pairs_in.reshape(half, 2, local_count, CAP, -1)

    placed = [
        embed(pairs_in[:, :, local].transpose(1, 0, 2, 3).reshape(slots, -1))
        for local in range(local_count)
    ]
    context_in = []
    for local in range(local_count):
        outgoing = spread(context, local)
        if local:
            outgoing, placed = lax.optimization_barrier((outgoing, placed))
        context_in.append(exchange(outgoing.reshape(devices, CAP, -1)).reshape(slots, -1))

    expert_ids, slot_ids, _ = lax.optimization_barrier((expert_ids, slot_ids, context))
    route_key = expert_ids * CAP + slot_ids
    stream_mid = (
        embedded.astype(jnp.float32) + jnp.dot(context, w_out, preferred_element_type=jnp.float32)
    ).astype(jnp.bfloat16)
    ffn_input = rms_scale(stream_mid.astype(jnp.float32), ffn_gain).astype(jnp.bfloat16)
    affinity = jax.nn.sigmoid(jnp.dot(ffn_input, router_w, preferred_element_type=jnp.float32))
    chosen_hot = expert_ids[:, :, None] == jnp.arange(experts, dtype=jnp.int32)[None, None, :]
    picked = jnp.sum(jnp.where(chosen_hot, affinity[:, None, :], 0.0), axis=-1)
    route_weight = picked / jnp.sum(picked, axis=1, keepdims=True)

    returned = []
    for local in range(local_count):
        mid = (
            placed[local].astype(jnp.float32)
            + jnp.dot(context_in[local], w_out, preferred_element_type=jnp.float32)
        ).astype(jnp.bfloat16)
        result = run_expert(mid, ffn_gain, expert_in, expert_out, local, local_count)
        if local == local_count - 1:
            result, stream_mid, route_weight = lax.optimization_barrier(
                (result, stream_mid, route_weight)
            )
        returned.append(exchange(result.reshape(devices, CAP, feat_dim)).reshape(slots, feat_dim))

    mixed = stream_mid.astype(jnp.float32)
    for local in range(local_count):
        kind = jnp.bfloat16 if local == local_count - 1 else jnp.float32
        mixed = combine(mixed, route_weight, route_key, row_keys[local], returned[local], kind)
    return mixed


def solution(mesh):
    placed = (
        P("tm", None),
        P(),
        P(),
        P(),
        P(),
        P(),
        P(),
        P(),
        P(),
        P(None, "tm", None),
        P("tm", None),
        P("tm", None),
        P("tm", None),
    )
    return jax.shard_map(
        shards, mesh=mesh, in_specs=placed, out_specs=P("tm", None), check_vma=False
    )
```

```python
import functools
import math

import jax
import jax.numpy as jnp
from jax import lax
from jax.experimental import pallas as pl
from jax.experimental.pallas import tpu as pltpu
from jax.sharding import PartitionSpec as P

HEAD_DIM = 128
WINDOW = 2048
CAP = 16

NORM_EPS = 1e-06
MASKED = -1e30


def from_behind(block, axis, distance):
    devices = range(lax.axis_size(axis))
    route = [(i - distance, i) for i in devices if i - distance in devices]
    return lax.ppermute(block, axis, route)


def rms_scale(values, gain_vec):
    mean_sq = jnp.mean(values * values, axis=-1, keepdims=True)
    return values * lax.rsqrt(mean_sq + NORM_EPS) * gain_vec


def head_norm(values):
    mean_sq = jnp.mean(values * values, axis=-1, keepdims=True)
    return values * lax.rsqrt(mean_sq + NORM_EPS)


def expert_body(steps, mid_ref, gain_ref, w_in_ref, w_out_ref, out_ref, rows_ref, total_ref):
    step = pl.program_id(1)

    @pl.when(step == 0)
    def _():
        mid = mid_ref[...].astype(jnp.float32)
        rows_ref[...] = rms_scale(mid, gain_ref[...]).astype(jnp.bfloat16)

    rows = rows_ref[...]
    nt = (((1,), (1,)), ((), ()))
    gate = lax.dot_general(rows, w_in_ref[0], nt, preferred_element_type=jnp.float32)
    up = lax.dot_general(rows, w_in_ref[1], nt, preferred_element_type=jnp.float32)
    hidden = (gate / (1.0 + jnp.exp(-gate)) * up).astype(jnp.bfloat16)
    part = jnp.dot(hidden, w_out_ref[...], preferred_element_type=jnp.float32)

    @pl.when(step == 0)
    def _():
        total_ref[...] = part

    @pl.when(step > 0)
    def _():
        total_ref[...] += part

    @pl.when(step == steps - 1)
    def _():
        out_ref[...] = total_ref[...].astype(out_ref.dtype)


def run_expert(mid, gain, expert_in, expert_out, local, local_count):
    row_total, feat_dim = mid.shape
    units = expert_out.shape[0] // local_count
    width = 704
    steps = units // width
    first = local * steps
    tile = math.gcd(row_total, 512)
    flops = 6 * row_total * units * feat_dim
    return pl.pallas_call(
        functools.partial(expert_body, steps),
        grid=(row_total // tile, steps),
        in_specs=[
            pl.BlockSpec((tile, feat_dim), lambda r, i: (r, 0)),
            pl.BlockSpec((1, feat_dim), lambda r, i: (0, 0)),
            pl.BlockSpec((2, width, feat_dim), lambda r, i: (0, first + i, 0)),
            pl.BlockSpec((width, feat_dim), lambda r, i: (first + i, 0)),
        ],
        out_specs=pl.BlockSpec((tile, feat_dim), lambda r, i: (r, 0)),
        out_shape=jax.ShapeDtypeStruct((row_total, feat_dim), jnp.bfloat16),
        scratch_shapes=[
            pltpu.VMEM((tile, feat_dim), jnp.bfloat16),
            pltpu.VMEM((tile, feat_dim), jnp.float32),
        ],
        compiler_params=pltpu.CompilerParams(vmem_limit_bytes=48 << 20),
        cost_estimate=pl.CostEstimate(
            flops=flops,
            bytes_accessed=6 * units * feat_dim + 4 * row_total * feat_dim,
            transcendentals=row_total * units,
        ),
    )(mid, gain.reshape(1, -1), expert_in, expert_out)


def spread_body(
    shape, info_ref, signal_ref, before_ref, key_ref, far_ref, out_ref
):
    half, copies, local_count, count = shape
    rows = out_ref.shape[0]
    tokens, width = signal_ref.shape
    first_dev, own_block = info_ref[0], info_ref[1]
    row = pl.program_id(0) * rows + lax.broadcasted_iota(jnp.int32, (rows, 1), 0)
    slot = lax.rem(row, CAP)
    local = lax.rem(lax.div(row, CAP), local_count)
    block = lax.rem(lax.div(row, CAP * local_count), 2)
    dev = first_dev + lax.div(row, CAP * local_count * 2)
    want = ((lax.div(dev, copies) * local_count + local) * CAP + slot).astype(jnp.float32)
    lane = lax.broadcasted_iota(jnp.int32, (8, tokens), 1)

    own_keys = [key_ref[route : route + 1].astype(jnp.float32) for route in range(2)]
    far_rows = [far_ref[tokens + 1 + at : tokens + 2 + at].astype(jnp.float32) for at in range(2)]
    far_all = far_rows[0] * CAP + far_rows[1]
    far_keys = [far_all[:, route * tokens : (route + 1) * tokens] for route in range(2)]
    far_before = far_ref[tokens : tokens + 1]
    now = jnp.zeros((rows, width), jnp.float32)
    past = jnp.zeros((rows, width), jnp.float32)
    for mine, keys, samples, before in (
        (True, own_keys, signal_ref[...], before_ref[...]),
        (False, far_keys, far_ref[:tokens], far_before),
    ):
        here = (block == own_block) if mine else (block != own_block)
        sought = jnp.where(here, want, -1.0)
        hot, hot_next, hot_first = False, False, False
        for key in keys:
            wide = jnp.broadcast_to(key, (8, tokens))
            after = jnp.where(lane == tokens - 1, -2.0, pltpu.roll(wide, tokens - 1, 1))[:1]
            hot = (sought == key) | hot
            hot_next = (sought == after) | hot_next
            hot_first = (sought == key[:, :1]) | hot_first
        now += jnp.dot(hot.astype(jnp.bfloat16), samples, preferred_element_type=jnp.float32)
        past += jnp.dot(
            hot_next.astype(jnp.bfloat16), samples, preferred_element_type=jnp.float32
        )
        past += jnp.where(hot_first, before.astype(jnp.float32), 0.0)
    out_ref[:, :width] = past.astype(out_ref.dtype)
    out_ref[:, width:] = now.astype(out_ref.dtype)


def spread_pairs(info, signal, before, keys, far, half, copies, local_count):
    tokens, width = signal.shape
    rows = half * 2 * local_count * CAP
    tile = math.gcd(rows, 256)
    whole = lambda shape: pl.BlockSpec(shape, lambda i: (0, 0))
    return pl.pallas_call(
        functools.partial(spread_body, (half, copies, local_count, tokens)),
        grid=(rows // tile,),
        in_specs=[
            pl.BlockSpec(memory_space=pltpu.SMEM),
            whole(signal.shape),
            whole(before.shape),
            whole(keys.shape),
            whole(far.shape),
        ],
        out_specs=pl.BlockSpec((tile, 2 * width), lambda i: (i, 0)),
        out_shape=jax.ShapeDtypeStruct((rows, 2 * width), jnp.bfloat16),
        compiler_params=pltpu.CompilerParams(vmem_limit_bytes=16 << 20),
        cost_estimate=pl.CostEstimate(
            flops=8 * rows * tokens * width,
            bytes_accessed=4 * rows * width + 4 * tokens * width,
            transcendentals=0,
        ),
    )(info, signal, before, keys, far)


def combine_body(base_ref, weight_ref, key_ref, row_ref, rows_ref, out_ref, hot_ref):
    @pl.when(pl.program_id(0) == 0)
    def _():
        for route in range(2):
            hot = key_ref[:, route : route + 1] == row_ref[...]
            hot_ref[route] = hot.astype(jnp.bfloat16)

    total = base_ref[...]
    for route in range(2):
        rows = jnp.dot(hot_ref[route], rows_ref[...], preferred_element_type=jnp.float32)
        rows = rows.astype(jnp.bfloat16).astype(jnp.float32)
        total = total + weight_ref[:, route : route + 1] * rows
    out_ref[...] = total.astype(out_ref.dtype)


def combine(base, weight, key, row_key, rows, kind):
    row_count, feat_dim = base.shape
    slots = rows.shape[0]
    width = math.gcd(feat_dim, 1024)
    return pl.pallas_call(
        combine_body,
        grid=(feat_dim // width,),
        in_specs=[
            pl.BlockSpec((row_count, width), lambda i: (0, i)),
            pl.BlockSpec((row_count, 2), lambda i: (0, 0)),
            pl.BlockSpec((row_count, 2), lambda i: (0, 0)),
            pl.BlockSpec((1, slots), lambda i: (0, 0)),
            pl.BlockSpec((slots, width), lambda i: (0, i)),
        ],
        out_specs=pl.BlockSpec((row_count, width), lambda i: (0, i)),
        out_shape=jax.ShapeDtypeStruct((row_count, feat_dim), kind),
        scratch_shapes=[pltpu.VMEM((2, row_count, slots), jnp.bfloat16)],
        compiler_params=pltpu.CompilerParams(vmem_limit_bytes=24 << 20),
        cost_estimate=pl.CostEstimate(
            flops=4 * row_count * slots * feat_dim,
            bytes_accessed=2 * slots * feat_dim + 8 * row_count * feat_dim,
            transcendentals=0,
        ),
    )(base, weight, key, row_key.reshape(1, -1), pltpu.with_memory_space_constraint(rows, pltpu.HBM))


def kv_body(rows_ref, weight_ref, out_ref):
    both = jnp.dot(rows_ref[...], weight_ref[...], preferred_element_type=jnp.float32)
    kv_dim = both.shape[1] // 2
    for start in range(0, kv_dim, HEAD_DIM):
        head = both[:, start : start + HEAD_DIM]
        out_ref[:, start : start + HEAD_DIM] = head_norm(head).astype(out_ref.dtype)
    out_ref[:, kv_dim:] = both[:, kv_dim:].astype(out_ref.dtype)


def project_kv(rows, weight):
    row_count, feat_dim = rows.shape
    width = weight.shape[1]
    return pl.pallas_call(
        kv_body,
        out_shape=jax.ShapeDtypeStruct((row_count, width), jnp.bfloat16),
        in_specs=[pl.BlockSpec(memory_space=pltpu.VMEM)] * 2,
        out_specs=pl.BlockSpec(memory_space=pltpu.VMEM),
        compiler_params=pltpu.CompilerParams(vmem_limit_bytes=16 << 20),
        cost_estimate=pl.CostEstimate(
            flops=2 * row_count * feat_dim * width,
            bytes_accessed=2 * (row_count * feat_dim + feat_dim * width),
            transcendentals=row_count,
        ),
    )(rows, weight)


def attend_body(kv_heads, flag_ref, scale_ref, query_ref, *refs):
    *kv_refs, out_ref, unit_ref, key_ref, value_ref, score_ref = refs
    blocks = [ref.at[part] for ref in kv_refs for part in range(ref.shape[0])]
    rows = query_ref.shape[0]
    heads = query_ref.shape[1] // HEAD_DIM
    group = heads // kv_heads
    kv_dim = kv_heads * HEAD_DIM
    count = len(blocks)
    for pos, block in enumerate(blocks):
        for kv in range(kv_heads):
            low = kv * HEAD_DIM
            key_ref[kv, pos] = block[:, low : low + HEAD_DIM]
            value_ref[kv, pos, :, :HEAD_DIM] = block[:, kv_dim + low : kv_dim + low + HEAD_DIM]
    for kv in range(kv_heads):
        for pos in range(count):
            value_ref[kv, pos, :, HEAD_DIM:] = jnp.ones((rows, HEAD_DIM), jnp.bfloat16)
    for head in range(heads):
        unit_ref[head] = head_norm(
            query_ref[:, head * HEAD_DIM : (head + 1) * HEAD_DIM]
        ).astype(jnp.bfloat16)
    query_at = lax.broadcasted_iota(jnp.int32, (rows, rows), 0)
    key_at = lax.broadcasted_iota(jnp.int32, (rows, rows), 1)

    @pl.loop(0, heads)
    def _(head):
        kv = head // group
        unit = unit_ref[head]
        top = jnp.full((rows, HEAD_DIM), MASKED, jnp.float32)
        for pos in range(count):
            score = lax.dot_general(
                unit,
                key_ref[kv, pos],
                (((1,), (1,)), ((), ())),
                preferred_element_type=jnp.float32,
            )
            if pos == 0:
                score = jnp.where(key_at <= query_at, score, MASKED)
            if pos == 1:
                score = jnp.where(key_at > query_at, score, MASKED)
            score_ref[pos] = score
            high = score[:, :HEAD_DIM]
            for low in range(HEAD_DIM, rows, HEAD_DIM):
                high = jnp.maximum(high, score[:, low : low + HEAD_DIM])
            if pos:
                high = jnp.where(flag_ref[pos] > 0, high, MASKED)
            top = jnp.maximum(top, high)
        factor = scale_ref[head] * (math.log2(math.e) / math.sqrt(HEAD_DIM))
        top = jnp.max(top, axis=1, keepdims=True)
        total = jnp.zeros((rows, 2 * HEAD_DIM), jnp.float32)
        for pos in range(count):
            base = jnp.where(flag_ref[pos] > 0, top, -MASKED) if pos else top
            weight = jnp.exp2((score_ref[pos] - base) * factor).astype(jnp.bfloat16)
            total += jnp.dot(weight, value_ref[kv, pos], preferred_element_type=jnp.float32)
        place_at = pl.ds(pl.multiple_of(head * HEAD_DIM, HEAD_DIM), HEAD_DIM)
        out_ref[:, place_at] = (total[:, :HEAD_DIM] / total[:, HEAD_DIM:]).astype(out_ref.dtype)


def attend(flags, head_scale, queries, kv_parts, kv_heads):
    rows, width = queries.shape
    heads = width // HEAD_DIM
    count = flags.shape[0]
    smem = pl.BlockSpec(memory_space=pltpu.SMEM)
    vmem = pl.BlockSpec(memory_space=pltpu.VMEM)
    return pl.pallas_call(
        functools.partial(attend_body, kv_heads),
        out_shape=jax.ShapeDtypeStruct((rows, width), jnp.bfloat16),
        in_specs=[smem, smem, vmem] + [vmem] * len(kv_parts),
        out_specs=vmem,
        scratch_shapes=[
            pltpu.VMEM((heads, rows, HEAD_DIM), jnp.bfloat16),
            pltpu.VMEM((kv_heads, count, rows, HEAD_DIM), jnp.bfloat16),
            pltpu.VMEM((kv_heads, count, rows, 2 * HEAD_DIM), jnp.bfloat16),
            pltpu.VMEM((count, rows, rows), jnp.float32),
        ],
        compiler_params=pltpu.CompilerParams(vmem_limit_bytes=32 << 20),
        cost_estimate=pl.CostEstimate(
            flops=6 * heads * count * rows * rows * HEAD_DIM,
            bytes_accessed=rows * width * 6 + count * rows * kv_heads * HEAD_DIM * 4,
            transcendentals=heads * count * rows * rows,
        ),
    )(flags, head_scale, queries, *kv_parts)


def window_parts(own_kv, prior_kv, group):
    devices = lax.axis_size("tm")
    me = lax.axis_index("tm")
    core, chip, base = me % 2, me % group // 2, me // group * group
    fetched, flags, sent = [], [], []
    for step in range(1, group // 2):
        other = chip ^ step
        block = jnp.where(other > chip, own_kv, prior_kv)
        sent.append(block)
        fetched.append(
            lax.ppermute(block, "tm", [(dev, dev ^ (2 * step)) for dev in range(devices)])
        )
        flags.append((other < chip) | (base > 0))
    shared = jnp.stack(fetched + [jnp.where(core == 0, own_kv, prior_kv)])
    shared = lax.ppermute(shared, "tm", [(dev, dev ^ 1) for dev in range(devices)])
    flags = [me >= 0, base > 0] + flags + flags + [(core > 0) | (base > 0)]
    parts = [block[None] for block in [own_kv, prior_kv] + fetched] + [shared]
    return parts, jnp.stack(flags).astype(jnp.int32), sent


def shards(
    signal,
    conv_weight,
    attn_gain,
    w_query,
    w_keyval,
    w_out,
    head_scale,
    ffn_gain,
    router_w,
    expert_in,
    expert_out,
    expert_ids,
    slot_ids,
):
    row_count = signal.shape[0]
    feat_dim = conv_weight.shape[1]
    devices = lax.axis_size("tm")
    dev_index = lax.axis_index("tm")
    experts = router_w.shape[1]
    copies = max(devices // experts, 1)
    local_count = max(experts // devices, 1)
    slots = devices * CAP

    route_key = expert_ids * CAP + slot_ids
    row_id = jnp.arange(slots, dtype=jnp.int32)
    row_dev, row_slot = row_id // CAP, row_id % CAP
    row_keys = [
        (row_dev // copies * local_count + local) * CAP + row_slot for local in range(local_count)
    ]

    def spread(values, local):
        hot = (row_keys[local][:, None] == route_key[None, :, 0]) | (
            row_keys[local][:, None] == route_key[None, :, 1]
        )
        return jnp.dot(
            hot.astype(jnp.bfloat16), values, preferred_element_type=jnp.float32
        ).astype(jnp.bfloat16)

    def exchange(rows):
        return lax.all_to_all(rows, "tm", split_axis=0, concat_axis=0, tiled=True)

    reach_blocks = WINDOW // row_count
    group = reach_blocks
    before = from_behind(signal[row_count - 1 :], "tm", 1)
    prior = from_behind(signal, "tm", group)
    prior_before = from_behind(signal[row_count - 1 :], "tm", group + 1)
    half = devices // 2
    routes = [
        table.astype(jnp.bfloat16).T.reshape(-1, signal.shape[1]) for table in (expert_ids, slot_ids)
    ]
    ahead = jnp.concatenate([signal, before] + routes, axis=0)
    ahead = jnp.pad(ahead, ((0, -ahead.shape[0] % 16), (0, 0)))
    far = lax.ppermute(ahead, "tm", [(dev, (dev + half) % devices) for dev in range(devices)])

    def pairs_of(block, first):
        return jnp.concatenate([jnp.concatenate([first, block[:-1]], axis=0), block], axis=1)

    def embed(pairs):
        rows = jnp.dot(pairs, conv_weight, preferred_element_type=jnp.float32)
        return rows.astype(jnp.bfloat16)

    def norm_rows(rows):
        return rms_scale(rows.astype(jnp.float32), attn_gain).astype(jnp.bfloat16)

    patch_pairs = pairs_of(signal, before)
    embedded = embed(patch_pairs)
    normed = norm_rows(embedded)
    kv_heads = w_keyval.shape[1] // 2 // HEAD_DIM
    own_kv = project_kv(normed, w_keyval)
    prior_pairs = pairs_of(prior, prior_before)
    prior_kv = project_kv(norm_rows(embed(prior_pairs)), w_keyval)
    kv_parts, flags, sent = window_parts(own_kv, prior_kv, group)
    queries = jnp.dot(normed, w_query, preferred_element_type=jnp.float32)
    context = attend(flags, head_scale, queries, kv_parts, kv_heads)

    far, _ = lax.optimization_barrier((far, sent))
    in_first = dev_index < half
    info = jnp.stack([jnp.where(in_first, 0, half), jnp.where(in_first, 0, 1)]).astype(jnp.int32)
    pairs_out = spread_pairs(info, signal, before, route_key.T, far, half, copies, local_count)
    pairs_out, _ = lax.optimization_barrier((pairs_out, kv_parts[2:-1]))
    pairs_in = lax.all_to_all(
        pairs_out.reshape(half, 2 * local_count * CAP, -1),
        "tm",
        split_axis=0,
        concat_axis=0,
        axis_index_groups=[list(range(half)), list(range(half, devices))],
        tiled=True,
    )
    pairs_in = pairs_in.reshape(half, 2, local_count, CAP, -1)

    placed = [
        embed(pairs_in[:, :, local].transpose(1, 0, 2, 3).reshape(slots, -1))
        for local in range(local_count)
    ]
    context_in = []
    for local in range(local_count):
        outgoing = spread(context, local)
        if local:
            outgoing, placed = lax.optimization_barrier((outgoing, placed))
        context_in.append(exchange(outgoing.reshape(devices, CAP, -1)).reshape(slots, -1))

    expert_ids, slot_ids, _ = lax.optimization_barrier((expert_ids, slot_ids, context))
    route_key = expert_ids * CAP + slot_ids
    stream_mid = (
        embedded.astype(jnp.float32) + jnp.dot(context, w_out, preferred_element_type=jnp.float32)
    ).astype(jnp.bfloat16)
    ffn_input = rms_scale(stream_mid.astype(jnp.float32), ffn_gain).astype(jnp.bfloat16)
    affinity = jax.nn.sigmoid(jnp.dot(ffn_input, router_w, preferred_element_type=jnp.float32))
    chosen_hot = expert_ids[:, :, None] == jnp.arange(experts, dtype=jnp.int32)[None, None, :]
    picked = jnp.sum(jnp.where(chosen_hot, affinity[:, None, :], 0.0), axis=-1)
    route_weight = picked / jnp.sum(picked, axis=1, keepdims=True)

    returned = []
    for local in range(local_count):
        mid = (
            placed[local].astype(jnp.float32)
            + jnp.dot(context_in[local], w_out, preferred_element_type=jnp.float32)
        ).astype(jnp.bfloat16)
        result = run_expert(mid, ffn_gain, expert_in, expert_out, local, local_count)
        if local == local_count - 1:
            result, stream_mid, route_weight = lax.optimization_barrier(
                (result, stream_mid, route_weight)
            )
        returned.append(exchange(result.reshape(devices, CAP, feat_dim)).reshape(slots, feat_dim))

    mixed = stream_mid.astype(jnp.float32)
    for local in range(local_count):
        kind = jnp.bfloat16 if local == local_count - 1 else jnp.float32
        mixed = combine(mixed, route_weight, route_key, row_keys[local], returned[local], kind)
    return mixed


def solution(mesh):
    placed = (
        P("tm", None),
        P(),
        P(),
        P(),
        P(),
        P(),
        P(),
        P(),
        P(),
        P(None, "tm", None),
        P("tm", None),
        P("tm", None),
        P("tm", None),
    )
    return jax.shard_map(
        shards, mesh=mesh, in_specs=placed, out_specs=P("tm", None), check_vma=False
    )
```

```python
import functools
import math

import jax
import jax.numpy as jnp
from jax import lax
from jax.experimental import pallas as pl
from jax.experimental.pallas import tpu as pltpu
from jax.sharding import PartitionSpec as P

HEAD_DIM = 128
WINDOW = 2048
CAP = 16

NORM_EPS = 1e-06
MASKED = -1e30


def from_behind(block, axis, distance):
    devices = range(lax.axis_size(axis))
    route = [(i - distance, i) for i in devices if i - distance in devices]
    return lax.ppermute(block, axis, route)


def rms_scale(values, gain_vec):
    mean_sq = jnp.mean(values * values, axis=-1, keepdims=True)
    return values * lax.rsqrt(mean_sq + NORM_EPS) * gain_vec


def head_norm(values):
    mean_sq = jnp.mean(values * values, axis=-1, keepdims=True)
    return values * lax.rsqrt(mean_sq + NORM_EPS)


def expert_body(steps, mid_ref, gain_ref, w_in_ref, w_out_ref, out_ref, rows_ref, total_ref):
    step = pl.program_id(1)

    @pl.when(step == 0)
    def _():
        mid = mid_ref[...].astype(jnp.float32)
        rows_ref[...] = rms_scale(mid, gain_ref[...]).astype(jnp.bfloat16)

    rows = rows_ref[...]
    nt = (((1,), (1,)), ((), ()))
    gate = lax.dot_general(rows, w_in_ref[0], nt, preferred_element_type=jnp.float32)
    up = lax.dot_general(rows, w_in_ref[1], nt, preferred_element_type=jnp.float32)
    hidden = (gate / (1.0 + jnp.exp(-gate)) * up).astype(jnp.bfloat16)
    part = jnp.dot(hidden, w_out_ref[...], preferred_element_type=jnp.float32)

    @pl.when(step == 0)
    def _():
        total_ref[...] = part

    @pl.when(step > 0)
    def _():
        total_ref[...] += part

    @pl.when(step == steps - 1)
    def _():
        out_ref[...] = total_ref[...].astype(out_ref.dtype)


def run_expert(mid, gain, expert_in, expert_out, local, local_count):
    row_total, feat_dim = mid.shape
    units = expert_out.shape[0] // local_count
    width = 704
    steps = units // width
    first = local * steps
    tile = math.gcd(row_total, 512)
    flops = 6 * row_total * units * feat_dim
    return pl.pallas_call(
        functools.partial(expert_body, steps),
        grid=(row_total // tile, steps),
        in_specs=[
            pl.BlockSpec((tile, feat_dim), lambda r, i: (r, 0)),
            pl.BlockSpec((1, feat_dim), lambda r, i: (0, 0)),
            pl.BlockSpec((2, width, feat_dim), lambda r, i: (0, first + i, 0)),
            pl.BlockSpec((width, feat_dim), lambda r, i: (first + i, 0)),
        ],
        out_specs=pl.BlockSpec((tile, feat_dim), lambda r, i: (r, 0)),
        out_shape=jax.ShapeDtypeStruct((row_total, feat_dim), jnp.bfloat16),
        scratch_shapes=[
            pltpu.VMEM((tile, feat_dim), jnp.bfloat16),
            pltpu.VMEM((tile, feat_dim), jnp.float32),
        ],
        compiler_params=pltpu.CompilerParams(vmem_limit_bytes=48 << 20),
        cost_estimate=pl.CostEstimate(
            flops=flops,
            bytes_accessed=6 * units * feat_dim + 4 * row_total * feat_dim,
            transcendentals=row_total * units,
        ),
    )(mid, gain.reshape(1, -1), expert_in, expert_out)


def spread_body(
    shape, info_ref, signal_ref, before_ref, key_ref, far_ref, out_ref
):
    half, copies, local_count, count = shape
    rows = out_ref.shape[0]
    tokens, width = signal_ref.shape
    first_dev, own_block = info_ref[0], info_ref[1]
    row = pl.program_id(0) * rows + lax.broadcasted_iota(jnp.int32, (rows, 1), 0)
    slot = lax.rem(row, CAP)
    local = lax.rem(lax.div(row, CAP), local_count)
    block = lax.rem(lax.div(row, CAP * local_count), 2)
    dev = first_dev + lax.div(row, CAP * local_count * 2)
    want = ((lax.div(dev, copies) * local_count + local) * CAP + slot).astype(jnp.float32)
    lane = lax.broadcasted_iota(jnp.int32, (8, tokens), 1)

    own_keys = [key_ref[route : route + 1].astype(jnp.float32) for route in range(2)]
    far_rows = [far_ref[tokens + 1 + at : tokens + 2 + at].astype(jnp.float32) for at in range(2)]
    far_all = far_rows[0] * CAP + far_rows[1]
    far_keys = [far_all[:, route * tokens : (route + 1) * tokens] for route in range(2)]
    far_before = far_ref[tokens : tokens + 1]
    now = jnp.zeros((rows, width), jnp.float32)
    past = jnp.zeros((rows, width), jnp.float32)
    for mine, keys, samples, before in (
        (True, own_keys, signal_ref[...], before_ref[...]),
        (False, far_keys, far_ref[:tokens], far_before),
    ):
        here = (block == own_block) if mine else (block != own_block)
        sought = jnp.where(here, want, -1.0)
        hot, hot_next, hot_first = False, False, False
        for key in keys:
            wide = jnp.broadcast_to(key, (8, tokens))
            after = jnp.where(lane == tokens - 1, -2.0, pltpu.roll(wide, tokens - 1, 1))[:1]
            hot = (sought == key) | hot
            hot_next = (sought == after) | hot_next
            hot_first = (sought == key[:, :1]) | hot_first
        now += jnp.dot(hot.astype(jnp.bfloat16), samples, preferred_element_type=jnp.float32)
        past += jnp.dot(
            hot_next.astype(jnp.bfloat16), samples, preferred_element_type=jnp.float32
        )
        past += jnp.where(hot_first, before.astype(jnp.float32), 0.0)
    out_ref[:, :width] = past.astype(out_ref.dtype)
    out_ref[:, width:] = now.astype(out_ref.dtype)


def spread_pairs(info, signal, before, keys, far, half, copies, local_count):
    tokens, width = signal.shape
    rows = half * 2 * local_count * CAP
    tile = math.gcd(rows, 256)
    whole = lambda shape: pl.BlockSpec(shape, lambda i: (0, 0))
    return pl.pallas_call(
        functools.partial(spread_body, (half, copies, local_count, tokens)),
        grid=(rows // tile,),
        in_specs=[
            pl.BlockSpec(memory_space=pltpu.SMEM),
            whole(signal.shape),
            whole(before.shape),
            whole(keys.shape),
            whole(far.shape),
        ],
        out_specs=pl.BlockSpec((tile, 2 * width), lambda i: (i, 0)),
        out_shape=jax.ShapeDtypeStruct((rows, 2 * width), jnp.bfloat16),
        compiler_params=pltpu.CompilerParams(vmem_limit_bytes=16 << 20),
        cost_estimate=pl.CostEstimate(
            flops=8 * rows * tokens * width,
            bytes_accessed=4 * rows * width + 4 * tokens * width,
            transcendentals=0,
        ),
    )(info, signal, before, keys, far)


def combine_body(base_ref, weight_ref, key_ref, row_ref, rows_ref, out_ref, hot_ref):
    @pl.when(pl.program_id(0) == 0)
    def _():
        for route in range(2):
            hot = key_ref[:, route : route + 1] == row_ref[...]
            hot_ref[route] = hot.astype(jnp.bfloat16)

    total = base_ref[...]
    for route in range(2):
        rows = jnp.dot(hot_ref[route], rows_ref[...], preferred_element_type=jnp.float32)
        rows = rows.astype(jnp.bfloat16).astype(jnp.float32)
        total = total + weight_ref[:, route : route + 1] * rows
    out_ref[...] = total.astype(out_ref.dtype)


def combine(base, weight, key, row_key, rows, kind):
    row_count, feat_dim = base.shape
    slots = rows.shape[0]
    width = math.gcd(feat_dim, 1024)
    return pl.pallas_call(
        combine_body,
        grid=(feat_dim // width,),
        in_specs=[
            pl.BlockSpec((row_count, width), lambda i: (0, i)),
            pl.BlockSpec((row_count, 2), lambda i: (0, 0)),
            pl.BlockSpec((row_count, 2), lambda i: (0, 0)),
            pl.BlockSpec((1, slots), lambda i: (0, 0)),
            pl.BlockSpec((slots, width), lambda i: (0, i)),
        ],
        out_specs=pl.BlockSpec((row_count, width), lambda i: (0, i)),
        out_shape=jax.ShapeDtypeStruct((row_count, feat_dim), kind),
        scratch_shapes=[pltpu.VMEM((2, row_count, slots), jnp.bfloat16)],
        compiler_params=pltpu.CompilerParams(vmem_limit_bytes=24 << 20),
        cost_estimate=pl.CostEstimate(
            flops=4 * row_count * slots * feat_dim,
            bytes_accessed=2 * slots * feat_dim + 8 * row_count * feat_dim,
            transcendentals=0,
        ),
    )(base, weight, key, row_key.reshape(1, -1), pltpu.with_memory_space_constraint(rows, pltpu.HBM))


def kv_body(rows_ref, weight_ref, out_ref):
    both = jnp.dot(rows_ref[...], weight_ref[...], preferred_element_type=jnp.float32)
    kv_dim = both.shape[1] // 2
    for start in range(0, kv_dim, HEAD_DIM):
        head = both[:, start : start + HEAD_DIM]
        out_ref[:, start : start + HEAD_DIM] = head_norm(head).astype(out_ref.dtype)
    out_ref[:, kv_dim:] = both[:, kv_dim:].astype(out_ref.dtype)


def project_kv(rows, weight):
    row_count, feat_dim = rows.shape
    width = weight.shape[1]
    return pl.pallas_call(
        kv_body,
        out_shape=jax.ShapeDtypeStruct((row_count, width), jnp.bfloat16),
        in_specs=[pl.BlockSpec(memory_space=pltpu.VMEM)] * 2,
        out_specs=pl.BlockSpec(memory_space=pltpu.VMEM),
        compiler_params=pltpu.CompilerParams(vmem_limit_bytes=16 << 20),
        cost_estimate=pl.CostEstimate(
            flops=2 * row_count * feat_dim * width,
            bytes_accessed=2 * (row_count * feat_dim + feat_dim * width),
            transcendentals=row_count,
        ),
    )(rows, weight)


def attend_body(kv_heads, flag_ref, scale_ref, query_ref, *refs):
    *kv_refs, out_ref, unit_ref, key_ref, value_ref, score_ref = refs
    blocks = [ref.at[part] for ref in kv_refs for part in range(ref.shape[0])]
    rows = query_ref.shape[0]
    heads = query_ref.shape[1] // HEAD_DIM
    group = heads // kv_heads
    kv_dim = kv_heads * HEAD_DIM
    count = len(blocks)
    for pos, block in enumerate(blocks):
        for kv in range(kv_heads):
            low = kv * HEAD_DIM
            key_ref[kv, pos] = block[:, low : low + HEAD_DIM]
            value_ref[kv, pos, :, :HEAD_DIM] = block[:, kv_dim + low : kv_dim + low + HEAD_DIM]
    for kv in range(kv_heads):
        for pos in range(count):
            value_ref[kv, pos, :, HEAD_DIM:] = jnp.ones((rows, HEAD_DIM), jnp.bfloat16)
    for head in range(heads):
        unit_ref[head] = head_norm(
            query_ref[:, head * HEAD_DIM : (head + 1) * HEAD_DIM]
        ).astype(jnp.bfloat16)
    query_at = lax.broadcasted_iota(jnp.int32, (rows, rows), 0)
    key_at = lax.broadcasted_iota(jnp.int32, (rows, rows), 1)

    @pl.loop(0, heads)
    def _(head):
        kv = head // group
        unit = unit_ref[head]
        top = jnp.full((rows, HEAD_DIM), MASKED, jnp.float32)
        for pos in range(count):
            score = lax.dot_general(
                unit,
                key_ref[kv, pos],
                (((1,), (1,)), ((), ())),
                preferred_element_type=jnp.float32,
            )
            if pos == 0:
                score = jnp.where(key_at <= query_at, score, MASKED)
            if pos == 1:
                score = jnp.where(key_at > query_at, score, MASKED)
            score_ref[pos] = score
            high = score[:, :HEAD_DIM]
            for low in range(HEAD_DIM, rows, HEAD_DIM):
                high = jnp.maximum(high, score[:, low : low + HEAD_DIM])
            if pos:
                high = jnp.where(flag_ref[pos] > 0, high, MASKED)
            top = jnp.maximum(top, high)
        factor = scale_ref[head] * (math.log2(math.e) / math.sqrt(HEAD_DIM))
        top = jnp.max(top, axis=1, keepdims=True)
        total = jnp.zeros((rows, 2 * HEAD_DIM), jnp.float32)
        for pos in range(count):
            base = jnp.where(flag_ref[pos] > 0, top, -MASKED) if pos else top
            weight = jnp.exp2((score_ref[pos] - base) * factor).astype(jnp.bfloat16)
            total += jnp.dot(weight, value_ref[kv, pos], preferred_element_type=jnp.float32)
        place_at = pl.ds(pl.multiple_of(head * HEAD_DIM, HEAD_DIM), HEAD_DIM)
        out_ref[:, place_at] = (total[:, :HEAD_DIM] / total[:, HEAD_DIM:]).astype(out_ref.dtype)


def attend(flags, head_scale, queries, kv_parts, kv_heads):
    rows, width = queries.shape
    heads = width // HEAD_DIM
    count = flags.shape[0]
    smem = pl.BlockSpec(memory_space=pltpu.SMEM)
    vmem = pl.BlockSpec(memory_space=pltpu.VMEM)
    return pl.pallas_call(
        functools.partial(attend_body, kv_heads),
        out_shape=jax.ShapeDtypeStruct((rows, width), jnp.bfloat16),
        in_specs=[smem, smem, vmem] + [vmem] * len(kv_parts),
        out_specs=vmem,
        scratch_shapes=[
            pltpu.VMEM((heads, rows, HEAD_DIM), jnp.bfloat16),
            pltpu.VMEM((kv_heads, count, rows, HEAD_DIM), jnp.bfloat16),
            pltpu.VMEM((kv_heads, count, rows, 2 * HEAD_DIM), jnp.bfloat16),
            pltpu.VMEM((count, rows, rows), jnp.float32),
        ],
        compiler_params=pltpu.CompilerParams(vmem_limit_bytes=32 << 20),
        cost_estimate=pl.CostEstimate(
            flops=6 * heads * count * rows * rows * HEAD_DIM,
            bytes_accessed=rows * width * 6 + count * rows * kv_heads * HEAD_DIM * 4,
            transcendentals=heads * count * rows * rows,
        ),
    )(flags, head_scale, queries, *kv_parts)


def window_parts(own_kv, prior_kv, group):
    devices = lax.axis_size("tm")
    me = lax.axis_index("tm")
    core, chip, base = me % 2, me % group // 2, me // group * group
    fetched, flags, sent = [], [], []
    for step in range(1, group // 2):
        other = chip ^ step
        block = jnp.where(other > chip, own_kv, prior_kv)
        sent.append(block)
        fetched.append(
            lax.ppermute(block, "tm", [(dev, dev ^ (2 * step)) for dev in range(devices)])
        )
        flags.append((other < chip) | (base > 0))
    shared = jnp.stack(fetched + [jnp.where(core == 0, own_kv, prior_kv)])
    shared = lax.ppermute(shared, "tm", [(dev, dev ^ 1) for dev in range(devices)])
    flags = [me >= 0, base > 0] + flags + flags + [(core > 0) | (base > 0)]
    parts = [block[None] for block in [own_kv, prior_kv] + fetched] + [shared]
    return parts, jnp.stack(flags).astype(jnp.int32), sent


def shards(
    signal,
    conv_weight,
    attn_gain,
    w_query,
    w_keyval,
    w_out,
    head_scale,
    ffn_gain,
    router_w,
    expert_in,
    expert_out,
    expert_ids,
    slot_ids,
):
    row_count = signal.shape[0]
    feat_dim = conv_weight.shape[1]
    devices = lax.axis_size("tm")
    dev_index = lax.axis_index("tm")
    experts = router_w.shape[1]
    copies = max(devices // experts, 1)
    local_count = max(experts // devices, 1)
    slots = devices * CAP

    route_key = expert_ids * CAP + slot_ids
    row_id = jnp.arange(slots, dtype=jnp.int32)
    row_dev, row_slot = row_id // CAP, row_id % CAP
    row_keys = [
        (row_dev // copies * local_count + local) * CAP + row_slot for local in range(local_count)
    ]

    def spread(values, local):
        hot = (row_keys[local][:, None] == route_key[None, :, 0]) | (
            row_keys[local][:, None] == route_key[None, :, 1]
        )
        return jnp.dot(
            hot.astype(jnp.bfloat16), values, preferred_element_type=jnp.float32
        ).astype(jnp.bfloat16)

    def exchange(rows):
        return lax.all_to_all(rows, "tm", split_axis=0, concat_axis=0, tiled=True)

    reach_blocks = WINDOW // row_count
    group = reach_blocks
    before = from_behind(signal[row_count - 1 :], "tm", 1)
    prior = from_behind(signal, "tm", group)
    prior_before = from_behind(signal[row_count - 1 :], "tm", group + 1)
    half = devices // 2
    routes = [
        table.astype(jnp.bfloat16).T.reshape(-1, signal.shape[1]) for table in (expert_ids, slot_ids)
    ]
    ahead = jnp.concatenate([signal, before] + routes, axis=0)
    ahead = jnp.pad(ahead, ((0, -ahead.shape[0] % 16), (0, 0)))
    far = lax.ppermute(ahead, "tm", [(dev, (dev + half) % devices) for dev in range(devices)])

    def pairs_of(block, first):
        return jnp.concatenate([jnp.concatenate([first, block[:-1]], axis=0), block], axis=1)

    def embed(pairs):
        rows = jnp.dot(pairs, conv_weight, preferred_element_type=jnp.float32)
        return rows.astype(jnp.bfloat16)

    def norm_rows(rows):
        return rms_scale(rows.astype(jnp.float32), attn_gain).astype(jnp.bfloat16)

    patch_pairs = pairs_of(signal, before)
    embedded = embed(patch_pairs)
    normed = norm_rows(embedded)
    kv_heads = w_keyval.shape[1] // 2 // HEAD_DIM
    own_kv = project_kv(normed, w_keyval)
    prior_pairs = pairs_of(prior, prior_before)
    prior_kv = project_kv(norm_rows(embed(prior_pairs)), w_keyval)
    kv_parts, flags, sent = window_parts(own_kv, prior_kv, group)
    queries = jnp.dot(normed, w_query, preferred_element_type=jnp.float32)
    context = attend(flags, head_scale, queries, kv_parts, kv_heads)

    far, _ = lax.optimization_barrier((far, sent))
    in_first = dev_index < half
    info = jnp.stack([jnp.where(in_first, 0, half), jnp.where(in_first, 0, 1)]).astype(jnp.int32)
    pairs_out = spread_pairs(info, signal, before, route_key.T, far, half, copies, local_count)
    pairs_out, _, _ = lax.optimization_barrier((pairs_out, kv_parts[2:-1], queries))
    pairs_in = lax.all_to_all(
        pairs_out.reshape(half, 2 * local_count * CAP, -1),
        "tm",
        split_axis=0,
        concat_axis=0,
        axis_index_groups=[list(range(half)), list(range(half, devices))],
        tiled=True,
    )
    pairs_in = pairs_in.reshape(half, 2, local_count, CAP, -1)

    placed = [
        embed(pairs_in[:, :, local].transpose(1, 0, 2, 3).reshape(slots, -1))
        for local in range(local_count)
    ]
    context_in = []
    for local in range(local_count):
        outgoing = spread(context, local)
        if local:
            outgoing, placed = lax.optimization_barrier((outgoing, placed))
        context_in.append(exchange(outgoing.reshape(devices, CAP, -1)).reshape(slots, -1))

    expert_ids, slot_ids, _ = lax.optimization_barrier((expert_ids, slot_ids, context))
    route_key = expert_ids * CAP + slot_ids
    stream_mid = (
        embedded.astype(jnp.float32) + jnp.dot(context, w_out, preferred_element_type=jnp.float32)
    ).astype(jnp.bfloat16)
    ffn_input = rms_scale(stream_mid.astype(jnp.float32), ffn_gain).astype(jnp.bfloat16)
    affinity = jax.nn.sigmoid(jnp.dot(ffn_input, router_w, preferred_element_type=jnp.float32))
    chosen_hot = expert_ids[:, :, None] == jnp.arange(experts, dtype=jnp.int32)[None, None, :]
    picked = jnp.sum(jnp.where(chosen_hot, affinity[:, None, :], 0.0), axis=-1)
    route_weight = picked / jnp.sum(picked, axis=1, keepdims=True)

    returned = []
    for local in range(local_count):
        mid = (
            placed[local].astype(jnp.float32)
            + jnp.dot(context_in[local], w_out, preferred_element_type=jnp.float32)
        ).astype(jnp.bfloat16)
        result = run_expert(mid, ffn_gain, expert_in, expert_out, local, local_count)
        if local == local_count - 1:
            result, stream_mid, route_weight = lax.optimization_barrier(
                (result, stream_mid, route_weight)
            )
        returned.append(exchange(result.reshape(devices, CAP, feat_dim)).reshape(slots, feat_dim))

    mixed = stream_mid.astype(jnp.float32)
    for local in range(local_count):
        kind = jnp.bfloat16 if local == local_count - 1 else jnp.float32
        mixed = combine(mixed, route_weight, route_key, row_keys[local], returned[local], kind)
    return mixed


def solution(mesh):
    placed = (
        P("tm", None),
        P(),
        P(),
        P(),
        P(),
        P(),
        P(),
        P(),
        P(),
        P(None, "tm", None),
        P("tm", None),
        P("tm", None),
        P("tm", None),
    )
    return jax.shard_map(
        shards, mesh=mesh, in_specs=placed, out_specs=P("tm", None), check_vma=False
    )
```

```python
import functools
import math

import jax
import jax.numpy as jnp
from jax import lax
from jax.experimental import pallas as pl
from jax.experimental.pallas import tpu as pltpu
from jax.sharding import PartitionSpec as P

HEAD_DIM = 128
WINDOW = 2048
CAP = 16

NORM_EPS = 1e-06
MASKED = -1e30


def from_behind(block, axis, distance):
    devices = range(lax.axis_size(axis))
    route = [(i - distance, i) for i in devices if i - distance in devices]
    return lax.ppermute(block, axis, route)


def rms_scale(values, gain_vec):
    mean_sq = jnp.mean(values * values, axis=-1, keepdims=True)
    return values * lax.rsqrt(mean_sq + NORM_EPS) * gain_vec


def head_norm(values):
    mean_sq = jnp.mean(values * values, axis=-1, keepdims=True)
    return values * lax.rsqrt(mean_sq + NORM_EPS)


def expert_body(steps, mid_ref, gain_ref, w_in_ref, w_out_ref, out_ref, rows_ref, total_ref):
    step = pl.program_id(1)

    @pl.when(step == 0)
    def _():
        mid = mid_ref[...].astype(jnp.float32)
        rows_ref[...] = rms_scale(mid, gain_ref[...]).astype(jnp.bfloat16)

    rows = rows_ref[...]
    nt = (((1,), (1,)), ((), ()))
    gate = lax.dot_general(rows, w_in_ref[0], nt, preferred_element_type=jnp.float32)
    up = lax.dot_general(rows, w_in_ref[1], nt, preferred_element_type=jnp.float32)
    hidden = (gate / (1.0 + jnp.exp(-gate)) * up).astype(jnp.bfloat16)
    part = jnp.dot(hidden, w_out_ref[...], preferred_element_type=jnp.float32)

    @pl.when(step == 0)
    def _():
        total_ref[...] = part

    @pl.when(step > 0)
    def _():
        total_ref[...] += part

    @pl.when(step == steps - 1)
    def _():
        out_ref[...] = total_ref[...].astype(out_ref.dtype)


def run_expert(mid, gain, expert_in, expert_out, local, local_count):
    row_total, feat_dim = mid.shape
    units = expert_out.shape[0] // local_count
    width = 704
    steps = units // width
    first = local * steps
    tile = math.gcd(row_total, 512)
    flops = 6 * row_total * units * feat_dim
    return pl.pallas_call(
        functools.partial(expert_body, steps),
        grid=(row_total // tile, steps),
        in_specs=[
            pl.BlockSpec((tile, feat_dim), lambda r, i: (r, 0)),
            pl.BlockSpec((1, feat_dim), lambda r, i: (0, 0)),
            pl.BlockSpec((2, width, feat_dim), lambda r, i: (0, first + i, 0)),
            pl.BlockSpec((width, feat_dim), lambda r, i: (first + i, 0)),
        ],
        out_specs=pl.BlockSpec((tile, feat_dim), lambda r, i: (r, 0)),
        out_shape=jax.ShapeDtypeStruct((row_total, feat_dim), jnp.bfloat16),
        scratch_shapes=[
            pltpu.VMEM((tile, feat_dim), jnp.bfloat16),
            pltpu.VMEM((tile, feat_dim), jnp.float32),
        ],
        compiler_params=pltpu.CompilerParams(vmem_limit_bytes=48 << 20),
        cost_estimate=pl.CostEstimate(
            flops=flops,
            bytes_accessed=6 * units * feat_dim + 4 * row_total * feat_dim,
            transcendentals=row_total * units,
        ),
    )(mid, gain.reshape(1, -1), expert_in, expert_out)


def spread_body(
    shape, info_ref, signal_ref, before_ref, key_ref, far_ref, out_ref
):
    half, copies, local_count, count = shape
    rows = out_ref.shape[0]
    tokens, width = signal_ref.shape
    first_dev, own_block = info_ref[0], info_ref[1]
    row = pl.program_id(0) * rows + lax.broadcasted_iota(jnp.int32, (rows, 1), 0)
    slot = lax.rem(row, CAP)
    local = lax.rem(lax.div(row, CAP), local_count)
    block = lax.rem(lax.div(row, CAP * local_count), 2)
    dev = first_dev + lax.div(row, CAP * local_count * 2)
    want = ((lax.div(dev, copies) * local_count + local) * CAP + slot).astype(jnp.float32)
    lane = lax.broadcasted_iota(jnp.int32, (8, tokens), 1)

    own_keys = [key_ref[route : route + 1].astype(jnp.float32) for route in range(2)]
    far_rows = [far_ref[tokens + 1 + at : tokens + 2 + at].astype(jnp.float32) for at in range(2)]
    far_all = far_rows[0] * CAP + far_rows[1]
    far_keys = [far_all[:, route * tokens : (route + 1) * tokens] for route in range(2)]
    far_before = far_ref[tokens : tokens + 1]
    now = jnp.zeros((rows, width), jnp.float32)
    past = jnp.zeros((rows, width), jnp.float32)
    for mine, keys, samples, before in (
        (True, own_keys, signal_ref[...], before_ref[...]),
        (False, far_keys, far_ref[:tokens], far_before),
    ):
        here = (block == own_block) if mine else (block != own_block)
        sought = jnp.where(here, want, -1.0)
        hot, hot_next, hot_first = False, False, False
        for key in keys:
            wide = jnp.broadcast_to(key, (8, tokens))
            after = jnp.where(lane == tokens - 1, -2.0, pltpu.roll(wide, tokens - 1, 1))[:1]
            hot = (sought == key) | hot
            hot_next = (sought == after) | hot_next
            hot_first = (sought == key[:, :1]) | hot_first
        now += jnp.dot(hot.astype(jnp.bfloat16), samples, preferred_element_type=jnp.float32)
        past += jnp.dot(
            hot_next.astype(jnp.bfloat16), samples, preferred_element_type=jnp.float32
        )
        past += jnp.where(hot_first, before.astype(jnp.float32), 0.0)
    out_ref[:, :width] = past.astype(out_ref.dtype)
    out_ref[:, width:] = now.astype(out_ref.dtype)


def spread_pairs(info, signal, before, keys, far, half, copies, local_count):
    tokens, width = signal.shape
    rows = half * 2 * local_count * CAP
    tile = math.gcd(rows, 256)
    whole = lambda shape: pl.BlockSpec(shape, lambda i: (0, 0))
    return pl.pallas_call(
        functools.partial(spread_body, (half, copies, local_count, tokens)),
        grid=(rows // tile,),
        in_specs=[
            pl.BlockSpec(memory_space=pltpu.SMEM),
            whole(signal.shape),
            whole(before.shape),
            whole(keys.shape),
            whole(far.shape),
        ],
        out_specs=pl.BlockSpec((tile, 2 * width), lambda i: (i, 0)),
        out_shape=jax.ShapeDtypeStruct((rows, 2 * width), jnp.bfloat16),
        compiler_params=pltpu.CompilerParams(vmem_limit_bytes=16 << 20),
        cost_estimate=pl.CostEstimate(
            flops=8 * rows * tokens * width,
            bytes_accessed=4 * rows * width + 4 * tokens * width,
            transcendentals=0,
        ),
    )(info, signal, before, keys, far)


def combine_body(base_ref, weight_ref, key_ref, row_ref, rows_ref, out_ref, hot_ref):
    @pl.when(pl.program_id(0) == 0)
    def _():
        for route in range(2):
            hot = key_ref[:, route : route + 1] == row_ref[...]
            hot_ref[route] = hot.astype(jnp.bfloat16)

    count, slots = hot_ref.shape[1:]
    both = jnp.dot(
        hot_ref[...].reshape(2 * count, slots), rows_ref[...], preferred_element_type=jnp.float32
    )
    total = base_ref[...]
    for route in range(2):
        rows = both[route * count : (route + 1) * count].astype(jnp.bfloat16)
        total = total + weight_ref[:, route : route + 1] * rows.astype(jnp.float32)
    out_ref[...] = total.astype(out_ref.dtype)


def combine(base, weight, key, row_key, rows, kind):
    row_count, feat_dim = base.shape
    slots = rows.shape[0]
    width = math.gcd(feat_dim, 1024)
    return pl.pallas_call(
        combine_body,
        grid=(feat_dim // width,),
        in_specs=[
            pl.BlockSpec((row_count, width), lambda i: (0, i)),
            pl.BlockSpec((row_count, 2), lambda i: (0, 0)),
            pl.BlockSpec((row_count, 2), lambda i: (0, 0)),
            pl.BlockSpec((1, slots), lambda i: (0, 0)),
            pl.BlockSpec((slots, width), lambda i: (0, i)),
        ],
        out_specs=pl.BlockSpec((row_count, width), lambda i: (0, i)),
        out_shape=jax.ShapeDtypeStruct((row_count, feat_dim), kind),
        scratch_shapes=[pltpu.VMEM((2, row_count, slots), jnp.bfloat16)],
        compiler_params=pltpu.CompilerParams(vmem_limit_bytes=24 << 20),
        cost_estimate=pl.CostEstimate(
            flops=4 * row_count * slots * feat_dim,
            bytes_accessed=2 * slots * feat_dim + 8 * row_count * feat_dim,
            transcendentals=0,
        ),
    )(base, weight, key, row_key.reshape(1, -1), pltpu.with_memory_space_constraint(rows, pltpu.HBM))


def kv_body(rows_ref, weight_ref, out_ref):
    both = jnp.dot(rows_ref[...], weight_ref[...], preferred_element_type=jnp.float32)
    kv_dim = both.shape[1] // 2
    for start in range(0, kv_dim, HEAD_DIM):
        head = both[:, start : start + HEAD_DIM]
        out_ref[:, start : start + HEAD_DIM] = head_norm(head).astype(out_ref.dtype)
    out_ref[:, kv_dim:] = both[:, kv_dim:].astype(out_ref.dtype)


def project_kv(rows, weight):
    row_count, feat_dim = rows.shape
    width = weight.shape[1]
    return pl.pallas_call(
        kv_body,
        out_shape=jax.ShapeDtypeStruct((row_count, width), jnp.bfloat16),
        in_specs=[pl.BlockSpec(memory_space=pltpu.VMEM)] * 2,
        out_specs=pl.BlockSpec(memory_space=pltpu.VMEM),
        compiler_params=pltpu.CompilerParams(vmem_limit_bytes=16 << 20),
        cost_estimate=pl.CostEstimate(
            flops=2 * row_count * feat_dim * width,
            bytes_accessed=2 * (row_count * feat_dim + feat_dim * width),
            transcendentals=row_count,
        ),
    )(rows, weight)


def attend_body(kv_heads, flag_ref, scale_ref, query_ref, *refs):
    *kv_refs, out_ref, unit_ref, key_ref, value_ref, score_ref = refs
    blocks = [ref.at[part] for ref in kv_refs for part in range(ref.shape[0])]
    rows = query_ref.shape[0]
    heads = query_ref.shape[1] // HEAD_DIM
    group = heads // kv_heads
    kv_dim = kv_heads * HEAD_DIM
    count = len(blocks)
    for pos, block in enumerate(blocks):
        for kv in range(kv_heads):
            low = kv * HEAD_DIM
            key_ref[kv, pos] = block[:, low : low + HEAD_DIM]
            value_ref[kv, pos, :, :HEAD_DIM] = block[:, kv_dim + low : kv_dim + low + HEAD_DIM]
    for kv in range(kv_heads):
        for pos in range(count):
            value_ref[kv, pos, :, HEAD_DIM:] = jnp.ones((rows, HEAD_DIM), jnp.bfloat16)
    for head in range(heads):
        unit_ref[head] = head_norm(
            query_ref[:, head * HEAD_DIM : (head + 1) * HEAD_DIM]
        ).astype(jnp.bfloat16)
    query_at = lax.broadcasted_iota(jnp.int32, (rows, rows), 0)
    key_at = lax.broadcasted_iota(jnp.int32, (rows, rows), 1)

    @pl.loop(0, heads)
    def _(head):
        kv = head // group
        unit = unit_ref[head]
        top = jnp.full((rows, HEAD_DIM), MASKED, jnp.float32)
        for pos in range(count):
            score = lax.dot_general(
                unit,
                key_ref[kv, pos],
                (((1,), (1,)), ((), ())),
                preferred_element_type=jnp.float32,
            )
            if pos == 0:
                score = jnp.where(key_at <= query_at, score, MASKED)
            if pos == 1:
                score = jnp.where(key_at > query_at, score, MASKED)
            score_ref[pos] = score
            high = score[:, :HEAD_DIM]
            for low in range(HEAD_DIM, rows, HEAD_DIM):
                high = jnp.maximum(high, score[:, low : low + HEAD_DIM])
            if pos:
                high = jnp.where(flag_ref[pos] > 0, high, MASKED)
            top = jnp.maximum(top, high)
        factor = scale_ref[head] * (math.log2(math.e) / math.sqrt(HEAD_DIM))
        top = jnp.max(top, axis=1, keepdims=True)
        total = jnp.zeros((rows, 2 * HEAD_DIM), jnp.float32)
        for pos in range(count):
            base = jnp.where(flag_ref[pos] > 0, top, -MASKED) if pos else top
            weight = jnp.exp2((score_ref[pos] - base) * factor).astype(jnp.bfloat16)
            total += jnp.dot(weight, value_ref[kv, pos], preferred_element_type=jnp.float32)
        place_at = pl.ds(pl.multiple_of(head * HEAD_DIM, HEAD_DIM), HEAD_DIM)
        out_ref[:, place_at] = (total[:, :HEAD_DIM] / total[:, HEAD_DIM:]).astype(out_ref.dtype)


def attend(flags, head_scale, queries, kv_parts, kv_heads):
    rows, width = queries.shape
    heads = width // HEAD_DIM
    count = flags.shape[0]
    smem = pl.BlockSpec(memory_space=pltpu.SMEM)
    vmem = pl.BlockSpec(memory_space=pltpu.VMEM)
    return pl.pallas_call(
        functools.partial(attend_body, kv_heads),
        out_shape=jax.ShapeDtypeStruct((rows, width), jnp.bfloat16),
        in_specs=[smem, smem, vmem] + [vmem] * len(kv_parts),
        out_specs=vmem,
        scratch_shapes=[
            pltpu.VMEM((heads, rows, HEAD_DIM), jnp.bfloat16),
            pltpu.VMEM((kv_heads, count, rows, HEAD_DIM), jnp.bfloat16),
            pltpu.VMEM((kv_heads, count, rows, 2 * HEAD_DIM), jnp.bfloat16),
            pltpu.VMEM((count, rows, rows), jnp.float32),
        ],
        compiler_params=pltpu.CompilerParams(vmem_limit_bytes=32 << 20),
        cost_estimate=pl.CostEstimate(
            flops=6 * heads * count * rows * rows * HEAD_DIM,
            bytes_accessed=rows * width * 6 + count * rows * kv_heads * HEAD_DIM * 4,
            transcendentals=heads * count * rows * rows,
        ),
    )(flags, head_scale, queries, *kv_parts)


def window_parts(own_kv, prior_kv, group):
    devices = lax.axis_size("tm")
    me = lax.axis_index("tm")
    core, chip, base = me % 2, me % group // 2, me // group * group
    fetched, flags, sent = [], [], []
    for step in range(1, group // 2):
        other = chip ^ step
        block = jnp.where(other > chip, own_kv, prior_kv)
        sent.append(block)
        fetched.append(
            lax.ppermute(block, "tm", [(dev, dev ^ (2 * step)) for dev in range(devices)])
        )
        flags.append((other < chip) | (base > 0))
    shared = jnp.stack(fetched + [jnp.where(core == 0, own_kv, prior_kv)])
    shared = lax.ppermute(shared, "tm", [(dev, dev ^ 1) for dev in range(devices)])
    flags = [me >= 0, base > 0] + flags + flags + [(core > 0) | (base > 0)]
    parts = [block[None] for block in [own_kv, prior_kv] + fetched] + [shared]
    return parts, jnp.stack(flags).astype(jnp.int32), sent


def shards(
    signal,
    conv_weight,
    attn_gain,
    w_query,
    w_keyval,
    w_out,
    head_scale,
    ffn_gain,
    router_w,
    expert_in,
    expert_out,
    expert_ids,
    slot_ids,
):
    row_count = signal.shape[0]
    feat_dim = conv_weight.shape[1]
    devices = lax.axis_size("tm")
    dev_index = lax.axis_index("tm")
    experts = router_w.shape[1]
    copies = max(devices // experts, 1)
    local_count = max(experts // devices, 1)
    slots = devices * CAP

    route_key = expert_ids * CAP + slot_ids
    row_id = jnp.arange(slots, dtype=jnp.int32)
    row_dev, row_slot = row_id // CAP, row_id % CAP
    row_keys = [
        (row_dev // copies * local_count + local) * CAP + row_slot for local in range(local_count)
    ]

    def spread(values, local):
        hot = (row_keys[local][:, None] == route_key[None, :, 0]) | (
            row_keys[local][:, None] == route_key[None, :, 1]
        )
        return jnp.dot(
            hot.astype(jnp.bfloat16), values, preferred_element_type=jnp.float32
        ).astype(jnp.bfloat16)

    def exchange(rows):
        return lax.all_to_all(rows, "tm", split_axis=0, concat_axis=0, tiled=True)

    reach_blocks = WINDOW // row_count
    group = reach_blocks
    before = from_behind(signal[row_count - 1 :], "tm", 1)
    prior = from_behind(signal, "tm", group)
    prior_before = from_behind(signal[row_count - 1 :], "tm", group + 1)
    half = devices // 2
    routes = [
        table.astype(jnp.bfloat16).T.reshape(-1, signal.shape[1]) for table in (expert_ids, slot_ids)
    ]
    ahead = jnp.concatenate([signal, before] + routes, axis=0)
    ahead = jnp.pad(ahead, ((0, -ahead.shape[0] % 16), (0, 0)))
    far = lax.ppermute(ahead, "tm", [(dev, (dev + half) % devices) for dev in range(devices)])

    def pairs_of(block, first):
        return jnp.concatenate([jnp.concatenate([first, block[:-1]], axis=0), block], axis=1)

    def embed(pairs):
        rows = jnp.dot(pairs, conv_weight, preferred_element_type=jnp.float32)
        return rows.astype(jnp.bfloat16)

    def norm_rows(rows):
        return rms_scale(rows.astype(jnp.float32), attn_gain).astype(jnp.bfloat16)

    patch_pairs = pairs_of(signal, before)
    embedded = embed(patch_pairs)
    normed = norm_rows(embedded)
    kv_heads = w_keyval.shape[1] // 2 // HEAD_DIM
    own_kv = project_kv(normed, w_keyval)
    prior_pairs = pairs_of(prior, prior_before)
    prior_kv = project_kv(norm_rows(embed(prior_pairs)), w_keyval)
    kv_parts, flags, sent = window_parts(own_kv, prior_kv, group)
    queries = jnp.dot(normed, w_query, preferred_element_type=jnp.float32)
    context = attend(flags, head_scale, queries, kv_parts, kv_heads)

    far, _ = lax.optimization_barrier((far, sent))
    in_first = dev_index < half
    info = jnp.stack([jnp.where(in_first, 0, half), jnp.where(in_first, 0, 1)]).astype(jnp.int32)
    pairs_out = spread_pairs(info, signal, before, route_key.T, far, half, copies, local_count)
    pairs_out, _, _ = lax.optimization_barrier((pairs_out, kv_parts[2:-1], queries))
    pairs_in = lax.all_to_all(
        pairs_out.reshape(half, 2 * local_count * CAP, -1),
        "tm",
        split_axis=0,
        concat_axis=0,
        axis_index_groups=[list(range(half)), list(range(half, devices))],
        tiled=True,
    )
    pairs_in = pairs_in.reshape(half, 2, local_count, CAP, -1)

    placed = [
        embed(pairs_in[:, :, local].transpose(1, 0, 2, 3).reshape(slots, -1))
        for local in range(local_count)
    ]
    context_in = []
    for local in range(local_count):
        outgoing = spread(context, local)
        if local:
            outgoing, placed = lax.optimization_barrier((outgoing, placed))
        context_in.append(exchange(outgoing.reshape(devices, CAP, -1)).reshape(slots, -1))

    expert_ids, slot_ids, _ = lax.optimization_barrier((expert_ids, slot_ids, context))
    route_key = expert_ids * CAP + slot_ids
    stream_mid = (
        embedded.astype(jnp.float32) + jnp.dot(context, w_out, preferred_element_type=jnp.float32)
    ).astype(jnp.bfloat16)
    ffn_input = rms_scale(stream_mid.astype(jnp.float32), ffn_gain).astype(jnp.bfloat16)
    affinity = jax.nn.sigmoid(jnp.dot(ffn_input, router_w, preferred_element_type=jnp.float32))
    chosen_hot = expert_ids[:, :, None] == jnp.arange(experts, dtype=jnp.int32)[None, None, :]
    picked = jnp.sum(jnp.where(chosen_hot, affinity[:, None, :], 0.0), axis=-1)
    route_weight = picked / jnp.sum(picked, axis=1, keepdims=True)

    returned = []
    for local in range(local_count):
        mid = (
            placed[local].astype(jnp.float32)
            + jnp.dot(context_in[local], w_out, preferred_element_type=jnp.float32)
        ).astype(jnp.bfloat16)
        result = run_expert(mid, ffn_gain, expert_in, expert_out, local, local_count)
        if local == local_count - 1:
            result, stream_mid, route_weight = lax.optimization_barrier(
                (result, stream_mid, route_weight)
            )
        returned.append(exchange(result.reshape(devices, CAP, feat_dim)).reshape(slots, feat_dim))

    mixed = stream_mid.astype(jnp.float32)
    for local in range(local_count):
        kind = jnp.bfloat16 if local == local_count - 1 else jnp.float32
        mixed = combine(mixed, route_weight, route_key, row_keys[local], returned[local], kind)
    return mixed


def solution(mesh):
    placed = (
        P("tm", None),
        P(),
        P(),
        P(),
        P(),
        P(),
        P(),
        P(),
        P(),
        P(None, "tm", None),
        P("tm", None),
        P("tm", None),
        P("tm", None),
    )
    return jax.shard_map(
        shards, mesh=mesh, in_specs=placed, out_specs=P("tm", None), check_vma=False
    )
```
